32 devices in a mesh: seq: 8 (over y, x, core), req: 4 (over z).
Axes of the slice: x: 2, y: 2, z: 4, core: 2. Of those that a mesh axis runs over, the one named last changes fastest.
Arguments:
- queries: bfloat16 [8, 256, 1536], P('req', 'seq'), as said below
- new_kv: bfloat16 [2, 8, 256, 512], P(None, 'req', 'seq'), may hold values from -6 to 6
- cache_kv: bfloat16 [2, 8, 2048, 512], P(None, 'req', 'seq'), as said below
- cache_spans: int32 [8, 2], P('req'), may hold values from 0 to 2048, as said below
- recompute_rows: int32 [8, 256], P('req'), may hold values from 0 to 2047, as said below
- held_states: bfloat16 [8, 256, 1536], P('req', 'seq'), may hold values from -6 to 6
- key_weight: bfloat16 [1536, 512], replicated, may hold values from -0.15625 to 0.15625
- norm_gain: float32 [1536], replicated, may hold values from 0.1 to 1.9
- routes: int32 [8, 256, 8], P('req', 'seq'), may hold values from 0 to 19, all different within a row; in each aligned block of 32 rows (0 to 31, 32 to 63, ..., all dimensions but the last counted through in order) at most 16 rows name the same one
- route_weights: float32 [8, 256, 8], P('req', 'seq'), may hold values from 0.05 to 1
- expert_gate_up: bfloat16 [20, 1536, 1024], P('req'), may hold values from -0.15625 to 0.15625
- expert_down: bfloat16 [20, 512, 1536], P('req'), may hold values from -0.25 to 0.25
Outputs:
- layer_out: bfloat16 [8, 256, 1536], P('req', 'seq')
The draws below stay inside these ranges and needn't reach their ends.
Inputs may be any that keep to these rules, and one draw needn't show every extreme that they name: `routes`: in each aligned block of 32 rows of one request (one device's rows of that request) no expert is named more than 16 times. cache_spans[r] = (start, length): 1024 <= length <= 2048 with some request of length 2048; 0 <= start <= 512 with some request starting at 0. `recompute_rows`: within a request the rows are distinct and lie between the request's start and length. `queries`: entries lie within -6 to 6. `cache_kv`: entries lie within -6 to 6.
All inputs are finite; a program needn't handle non-finite values.
Results may differ from the reference program's by a relative error of at most 0.034.
Values may be sent and summed in bfloat16 or wider, within the bound.
A program may use at most 192 MiB of HBM per device.

```python
import math
import jax
import jax.numpy as jnp
import numpy as np
from jax import lax

D = 1536
H = 24
KVH = 8
HD = 64
FF = 512
TOP = 8
STEP_DEV = 32
CAP = 16
EXPERTS = 20
REQUESTS = 8
STEP = 256
CACHE = 2048
RECOMP = 256


def draw_queries(key, part):
    values = jnp.clip(jax.random.normal(jax.random.fold_in(key, 1), (REQUESTS, STEP, H * HD), jnp.float32), -4.0, 4.0)
    return values.astype(jnp.bfloat16)


def draw_cache_kv(key, part):
    values = jnp.clip(jax.random.normal(jax.random.fold_in(key, 2), (2, REQUESTS, CACHE, KVH * HD), jnp.float32), -4.0, 4.0)
    return values.astype(jnp.bfloat16)


def span_table(key):
    folded = jax.random.fold_in(key, 5)
    key_length, key_pick, key_start, key_zero = jax.random.split(folded, 4)
    lengths = jax.random.randint(key_length, (REQUESTS,), CACHE // 2, CACHE + 1)
    lengths = jnp.where(jnp.arange(REQUESTS) == jax.random.randint(key_pick, (), 0, REQUESTS), CACHE, lengths)
    starts = jax.random.randint(key_start, (REQUESTS,), 0, CACHE // 4 + 1)
    starts = jnp.where(jnp.arange(REQUESTS) == jax.random.randint(key_zero, (), 0, REQUESTS), 0, starts)
    return (starts, lengths)


def draw_cache_spans(key, part):
    starts, lengths = span_table(key)
    return jnp.stack([starts, lengths], axis=1).astype(jnp.int32)


def draw_recompute_rows(key, part):
    starts, lengths = span_table(key)
    stride = (lengths - starts) // RECOMP
    offsets = jax.random.randint(jax.random.fold_in(key, 9), (REQUESTS, RECOMP), 0, 1 << 20) % stride[:, None]
    rows = starts[:, None] + jnp.arange(RECOMP)[None, :] * stride[:, None] + offsets
    column = jnp.arange(RECOMP)[None, :]
    rows = jnp.where(column == 0, starts[:, None], rows)
    rows = jnp.where(column == RECOMP - 1, lengths[:, None] - 1, rows)
    return rows.astype(jnp.int32)


def block_scale(key, dims, shards, low, high):
    factor_of = 1.0
    for dim, blocks in shards:
        steps = jax.random.uniform(jax.random.fold_in(jax.random.fold_in(key, 6), dim), (blocks,), jnp.float32, low / len(shards), high / len(shards))
        factor_of = factor_of * jnp.repeat(jnp.exp(steps), dims[dim] // blocks).reshape((-1,) + (1,) * (len(dims) - 1 - dim))
    return factor_of


def routed_block(stream_key, own, number, rows, amount, top, bound, skew):
    order = jax.random.permutation(stream_key, amount)
    crowded, usual = shares(amount, rows * top, bound, skew, True), shares(amount, rows * top, bound, skew, False)
    places = jnp.arange(amount)

    def named(tallies, rotation):
        used = int((tallies > 0).sum())
        fixed = max(1, used // 4)
        shifted = fixed + (places - fixed + rotation * (used - fixed)) % max(1, amount - fixed)
        return jnp.zeros((amount,), jnp.int32).at[order[jnp.where(places < fixed, places, shifted)]].set(jnp.asarray(tallies, jnp.int32))

    tallies = jnp.where(number % 4 == 0, named(crowded, number // 4), named(usual, number - number // 4 - 1))
    mixed = jax.random.permutation(jax.random.fold_in(own, 3), amount)
    giver, sink = mixed[0:amount // 2 * 2:2], mixed[1:amount // 2 * 2:2]
    room = jnp.minimum(tallies[giver] - 1, bound - tallies[sink]) // 2
    room = jnp.where((giver == order[0]) | (sink == order[0]) | (tallies[sink] == 0), 0, jnp.maximum(room, 0))
    shifted = jax.random.randint(jax.random.fold_in(own, 4), (amount // 2,), 0, 1 << 20) % (room + 1)
    tallies = tallies.at[giver].add(-shifted).at[sink].add(shifted)
    members = jnp.searchsorted(jnp.cumsum(tallies), jnp.arange(rows * top), side="right").astype(jnp.int32)
    grid = members.reshape(top, rows).T
    grid = grid[jax.random.permutation(jax.random.fold_in(own, 1), rows)]
    rotation = jax.random.randint(jax.random.fold_in(own, 2), (rows, 1), 0, top)
    return jnp.take_along_axis(grid, (jnp.arange(top)[None, :] + rotation) % top, axis=1)


def shares(count, total, reach, skew, full):
    loads = [(1 << 20) // math.isqrt(standing ** skew) + 1 for standing in range(1, count + 1)]
    largest = reach if full else min(reach, max(-(-total // count), total * loads[0] // sum(loads)))
    least = 1 if total - largest >= count - 1 else 0
    holding, surplus = [largest] + [least] * (count - 1), total - largest - least * (count - 1)
    while surplus > 0:
        candidates = [i for i in range(1, count) if holding[i] < largest] or [i for i in range(1, count) if holding[i] < reach]
        pool, budget = sum([loads[i] for i in candidates]), surplus
        for i in candidates:
            addition = min(reach - holding[i], max(1, budget * loads[i] // pool), surplus)
            holding[i] = holding[i] + addition
            surplus = surplus - addition
    return np.array(holding)


def noise(key, extent, scale, limit, cuts=(), kind=jnp.bfloat16):
    array = jax.random.normal(key, extent, jnp.float32) * scale
    if len(cuts) > 0:
        array = block_scale(key, extent, cuts, -0.22, 0.18) * array
    return jnp.clip(array, min=-limit, max=limit).astype(kind)


def setup_inputs(seed: int = 0) -> dict:
    streams_of = jax.random.split(jax.random.key(seed), 13)
    queries = draw_queries(jax.random.fold_in(streams_of[12], 71), 0)
    new_kv = noise(streams_of[1], (2, REQUESTS, STEP, KVH * HD), 1.0, 6.0, ((1, 4), (2, 8)))
    cache_kv = draw_cache_kv(jax.random.fold_in(streams_of[12], 71), 0)
    cache_spans = draw_cache_spans(jax.random.fold_in(streams_of[12], 71), 0)
    recompute_rows = draw_recompute_rows(jax.random.fold_in(streams_of[12], 71), 0)
    held_states = noise(streams_of[5], (REQUESTS, RECOMP, D), 1.0, 6.0, ((0, 4), (1, 8)))
    key_weight = noise(streams_of[6], (D, KVH * HD), D ** -0.5, 0.15625)
    norm_gain = jnp.clip(1.0 + 0.18 * jax.random.normal(streams_of[7], (D,), jnp.float32), 0.1, 1.9)
    routes_keys = jax.random.split(jax.random.fold_in(streams_of[8], 1), REQUESTS * STEP // STEP_DEV)
    routes_turns = jax.random.permutation(jax.random.fold_in(streams_of[8], 3), REQUESTS * STEP // STEP_DEV)
    routes = jax.vmap(lambda own, number: routed_block(jax.random.fold_in(streams_of[8], 2), own, number, STEP_DEV, EXPERTS, TOP, CAP, 1))(routes_keys, routes_turns).reshape((REQUESTS, STEP, TOP))
    route_weights = jnp.clip(0.05 + 0.95 * jax.random.uniform(streams_of[9], (REQUESTS, STEP, TOP), jnp.float32) ** block_scale(streams_of[9], (REQUESTS, STEP, TOP), ((0, 4), (1, 8)), -0.2, 0.2), 0.05, 1.0)
    expert_gate_up = noise(streams_of[10], (EXPERTS, D, 2 * FF), D ** -0.5, 0.15625, ((0, 4),))
    expert_down = noise(streams_of[11], (EXPERTS, FF, D), FF ** -0.5, 0.25, ((0, 4),))
    return {"queries": queries, "new_kv": new_kv, "cache_kv": cache_kv, "cache_spans": cache_spans, "recompute_rows": recompute_rows, "held_states": held_states, "key_weight": key_weight, "norm_gain": norm_gain, "routes": routes, "route_weights": route_weights, "expert_gate_up": expert_gate_up, "expert_down": expert_down}


NEG = -1e+30
THETA = 10000.0

def rotate(key_heads, positions):
    half_dim = key_heads.shape[-1] // 2
    exponent = jnp.arange(half_dim).astype(jnp.float32) * (2.0 / key_heads.shape[-1])
    inverse = THETA ** (-exponent)
    angles = positions.astype(jnp.float32)[..., None] * inverse
    cosine = jnp.cos(angles)[..., None, :]
    sine_part = jnp.sin(angles)[..., None, :]
    lower_half = key_heads[..., :half_dim]
    upper_half = key_heads[..., half_dim:]
    return jnp.concatenate([lower_half * cosine - upper_half * sine_part, upper_half * cosine + lower_half * sine_part], axis=-1)

def attend_request(packed):
    query_rows, cache_key_rows, cache_value_rows, step_key_rows, step_value_rows, span_pair = packed
    groups = H // KVH
    key_heads = jnp.concatenate([cache_key_rows, step_key_rows], axis=0).astype(jnp.float32).reshape(CACHE + STEP, KVH, HD)
    value_heads = jnp.concatenate([cache_value_rows, step_value_rows], axis=0).astype(jnp.float32).reshape(CACHE + STEP, KVH, HD)
    query_heads = query_rows.astype(jnp.float32).reshape(STEP, KVH, groups, HD)
    scores = jnp.einsum('qkgd,nkd->kgqn', query_heads, key_heads, precision=lax.Precision.HIGHEST) * HD ** (-0.5)
    cache_index = jnp.arange(CACHE).astype(jnp.int32)
    cache_allowed = (cache_index >= span_pair[0]) & (cache_index < span_pair[1])
    step_index = jnp.arange(STEP).astype(jnp.int32)
    step_allowed = step_index[None, :] <= step_index[:, None]
    allowed = jnp.concatenate([jnp.broadcast_to(cache_allowed[None, :], (STEP, CACHE)), step_allowed], axis=1)
    scores = jnp.where(allowed[None, None], scores, NEG)
    highest = lax.optimization_barrier(jnp.max(scores, axis=-1, keepdims=True))
    exps = jnp.exp(scores - highest)
    totals = lax.optimization_barrier(jnp.sum(exps, axis=-1))
    weights = lax.optimization_barrier(exps.astype(jnp.bfloat16)).astype(jnp.float32)
    mixed_rows = jnp.einsum('kgqn,nkd->qkgd', weights, value_heads, precision=lax.Precision.HIGHEST)
    mixed_rows = mixed_rows / jnp.transpose(totals, (2, 0, 1))[..., None]
    return mixed_rows.reshape(STEP, D).astype(jnp.bfloat16)

def expert_outputs(normed, routes, expert_gate_up, expert_down):
    tile_rows = 256
    token_total = normed.shape[0] * normed.shape[1]
    flat_tokens = jnp.concatenate([normed.reshape(token_total, D), jnp.zeros((1, D), normed.dtype)], axis=0)
    flat_routes = routes.reshape(-1).astype(jnp.int32)
    route_total = flat_routes.shape[0]
    owner_token = (jnp.arange(route_total) // TOP).astype(jnp.int32)
    counts = lax.optimization_barrier(jnp.sum((flat_routes[:, None] == jnp.arange(EXPERTS).astype(jnp.int32)[None, :]).astype(jnp.int32), axis=0)).astype(jnp.int32)
    padded = ((counts + tile_rows - 1) // tile_rows * tile_rows).astype(jnp.int32)
    padded_start = (jnp.cumsum(padded) - padded).astype(jnp.int32)
    first_sorted = (jnp.cumsum(counts) - counts).astype(jnp.int32)
    sort_order = jnp.argsort(flat_routes, stable=True).astype(jnp.int32)
    sorted_experts = flat_routes[sort_order]
    rank_within = (jnp.arange(route_total).astype(jnp.int32) - first_sorted[sorted_experts]).astype(jnp.int32)
    destination = (padded_start[sorted_experts] + rank_within).astype(jnp.int32)
    block_count = (route_total + tile_rows - 1) // tile_rows + EXPERTS
    slot_token = jnp.full((block_count * tile_rows,), token_total, jnp.int32).at[destination].set(owner_token[sort_order])
    block_starts = (jnp.arange(block_count) * tile_rows).astype(jnp.int32)
    block_expert = (lax.optimization_barrier(jnp.sum((padded_start[None, :] <= block_starts[:, None]).astype(jnp.int32), axis=1)) - 1).astype(jnp.int32)

    def one_block(packed):
        token_ids, expert_id = packed
        row_block = flat_tokens[token_ids]
        hidden = jnp.dot(row_block, expert_gate_up[expert_id], preferred_element_type=jnp.float32)
        active = (jax.nn.silu(hidden[:, :FF]) * hidden[:, FF:]).astype(jnp.bfloat16)
        return jnp.dot(active, expert_down[expert_id], preferred_element_type=jnp.float32).astype(jnp.bfloat16)
    outputs = lax.map(one_block, (slot_token.reshape(block_count, tile_rows), block_expert))
    outputs = outputs.reshape(block_count * tile_rows, D)
    position = jnp.zeros((route_total,), jnp.int32).at[sort_order].set(destination)
    return outputs[position].reshape(normed.shape[0], normed.shape[1], TOP, D)

def reference(queries, new_kv, cache_kv, cache_spans, recompute_rows, held_states, key_weight, norm_gain, routes, route_weights, expert_gate_up, expert_down):
    projected = jnp.dot(held_states.reshape(REQUESTS * RECOMP, D), key_weight, preferred_element_type=jnp.float32)
    rotated = rotate(projected.reshape(REQUESTS, RECOMP, KVH, HD), recompute_rows)
    fresh_rows = rotated.reshape(REQUESTS, RECOMP, KVH * HD).astype(jnp.bfloat16)
    request_ids = jnp.arange(REQUESTS).astype(jnp.int32)[:, None]
    cache_keys = cache_kv[0].at[request_ids, recompute_rows.astype(jnp.int32)].set(fresh_rows)
    attended = lax.map(attend_request, (queries, cache_keys, cache_kv[1], new_kv[0], new_kv[1], cache_spans))
    attended_f = attended.astype(jnp.float32)
    mean_square = lax.optimization_barrier(jnp.mean(attended_f * attended_f, axis=-1, keepdims=True))
    normed = (attended_f * lax.rsqrt(mean_square + 1e-06) * norm_gain).astype(jnp.bfloat16)
    routed = expert_outputs(normed, routes, expert_gate_up, expert_down)
    mixture = jnp.einsum('rtk,rtkd->rtd', route_weights, routed.astype(jnp.float32), precision=lax.Precision.HIGHEST)
    return (attended_f + mixture).astype(jnp.bfloat16)
```

```python
import jax
import jax.numpy as jnp
import numpy as np
from jax import lax
from jax.experimental import pallas as pl
from jax.experimental.pallas import tpu as pltpu
from jax.sharding import PartitionSpec as P

H = 24
KVH = 8
HD = 64
FF = 512
TOP = 8
CAP = 16


NEG = -1e30
THETA = 10000.0


def rotate(key_heads, positions):
    half_dim = key_heads.shape[-1] // 2
    exponent = jnp.arange(half_dim).astype(jnp.float32) * (2.0 / key_heads.shape[-1])
    inverse = THETA ** (-exponent)
    angles = positions.astype(jnp.float32)[..., None] * inverse
    cosine = jnp.cos(angles)[..., None, :]
    sine_part = jnp.sin(angles)[..., None, :]
    lower_half = key_heads[..., :half_dim]
    upper_half = key_heads[..., half_dim:]
    return jnp.concatenate(
        [
            lower_half * cosine - upper_half * sine_part,
            upper_half * cosine + lower_half * sine_part,
        ],
        axis=-1,
    )


def partial_attend(packed):
    query_rows, key_rows, value_rows, allowed = packed
    query_count, model_width = query_rows.shape
    key_count = key_rows.shape[0]
    groups = H // KVH
    query_heads = query_rows.reshape(query_count, KVH, groups, HD)
    key_heads = key_rows.reshape(key_count, KVH, HD)
    value_heads = value_rows.reshape(key_count, KVH, HD)
    scores = jnp.einsum(
        "qkgd,nkd->kgqn", query_heads, key_heads, preferred_element_type=jnp.float32
    ) * HD ** (-0.5)
    scores = jnp.where(allowed[None, None, :, :], scores, NEG)
    highest = jnp.max(scores, axis=-1, keepdims=True)
    exps = jnp.exp(scores - highest)
    totals = jnp.sum(exps, axis=-1)
    weights = exps.astype(jnp.bfloat16)
    mixed_rows = jnp.einsum(
        "kgqn,nkd->qkgd", weights, value_heads, preferred_element_type=jnp.float32
    )
    mixed_rows = mixed_rows / jnp.transpose(totals, (2, 0, 1))[..., None]
    log_total = highest[..., 0] + jnp.log(totals)
    log_rows = jnp.transpose(log_total, (2, 0, 1)).reshape(query_count, H)
    return (mixed_rows.reshape(query_count, model_width), log_rows)


def body_wide(
    queries,
    new_kv,
    cache_kv,
    cache_spans,
    recompute_rows,
    held_states,
    key_weight,
    norm_gain,
    routes,
    route_weights,
    expert_gate_up,
    expert_down,
):
    seq_index = lax.axis_index("seq")
    seq_count = lax.axis_size("seq")
    owner_count = lax.axis_size("req")
    req_rows, tok_rows, model_width = queries.shape
    cache_rows = cache_kv.shape[2]
    held_rows = held_states.shape[1]
    local_experts = expert_gate_up.shape[0]
    expert_total = owner_count * local_experts
    my_positions = lax.dynamic_slice_in_dim(recompute_rows, seq_index * held_rows, held_rows, 1)
    projected = jnp.dot(
        held_states.reshape(req_rows * held_rows, model_width),
        key_weight,
        preferred_element_type=jnp.float32,
    )
    rotated = rotate(projected.reshape(req_rows, held_rows, KVH, HD), my_positions)
    rotated = rotated.reshape(req_rows, held_rows, KVH * HD).astype(jnp.bfloat16)
    fresh_rows = lax.all_gather(rotated, "seq", axis=1, tiled=True)
    cache_positions = seq_index * cache_rows + jnp.arange(cache_rows)
    hit_table = recompute_rows[:, None, :] == cache_positions[None, :, None]
    placed = jnp.einsum(
        "rcm,rmk->rck",
        hit_table.astype(jnp.bfloat16),
        fresh_rows,
        preferred_element_type=jnp.float32,
    ).astype(jnp.bfloat16)
    cache_keys = jnp.where(jnp.any(hit_table, axis=2)[:, :, None], placed, cache_kv[0])
    span_start = cache_spans[:, 0:1]
    span_end = cache_spans[:, 1:2]
    all_queries = lax.all_gather(queries, "seq", axis=1, tiled=True)
    step_total = all_queries.shape[1]
    cache_allowed = (cache_positions[None, :] >= span_start) & (cache_positions[None, :] < span_end)
    key_positions = seq_index * tok_rows + jnp.arange(tok_rows)
    step_allowed = key_positions[None, :] <= jnp.arange(step_total)[:, None]
    allowed = jnp.concatenate(
        [
            jnp.broadcast_to(cache_allowed[:, None, :], (req_rows, step_total, cache_rows)),
            jnp.broadcast_to(step_allowed[None], (req_rows, step_total, tok_rows)),
        ],
        axis=2,
    )
    key_rows = jnp.concatenate([cache_keys, new_kv[0]], axis=1)
    value_rows = jnp.concatenate([cache_kv[1], new_kv[1]], axis=1)
    part_out, part_log = lax.map(partial_attend, (all_queries, key_rows, value_rows, allowed))
    piece_out, piece_log = (
        lax.all_to_all(part_out[None], "seq", split_axis=2, concat_axis=0, tiled=True),
        lax.all_to_all(part_log[None], "seq", split_axis=2, concat_axis=0, tiled=True),
    )
    best_log = jnp.max(piece_log, axis=0)
    factors = jnp.exp(piece_log - best_log[None])
    factor_sum = jnp.sum(factors, axis=0)
    spread_out = piece_out.reshape(seq_count, req_rows, tok_rows, H, HD)
    combined = jnp.sum(spread_out * factors[..., None], axis=0) / factor_sum[..., None]
    attended_f = combined.reshape(req_rows, tok_rows, model_width)
    attended = attended_f.astype(jnp.bfloat16)
    attended_f = attended.astype(jnp.float32)
    mean_square = jnp.mean(attended_f * attended_f, axis=-1, keepdims=True)
    normed = (attended_f * lax.rsqrt(mean_square + 1e-06) * norm_gain).astype(jnp.bfloat16)
    route_flat = routes.reshape(req_rows, tok_rows * TOP)
    expert_match = (route_flat[:, :, None] == jnp.arange(expert_total)[None, None, :]).astype(
        jnp.int32
    )
    order = jnp.arange(tok_rows * TOP)
    before = (order[None, :] < order[:, None]).astype(jnp.bfloat16)
    earlier = jnp.einsum(
        "ij,rje->rie",
        before,
        expert_match.astype(jnp.bfloat16),
        preferred_element_type=jnp.float32,
    ).astype(jnp.int32)
    slot_index = jnp.sum(earlier * expert_match, axis=2)
    target = route_flat * CAP + slot_index
    slot_match = target[:, :, None] == jnp.arange(expert_total * CAP)[None, None, :]
    dispatch = jnp.any(
        slot_match.reshape(req_rows, tok_rows, TOP, expert_total * CAP), axis=2
    ).astype(jnp.bfloat16)
    dispatch = dispatch.reshape(req_rows, tok_rows, owner_count, local_experts, CAP)
    outgoing = jnp.einsum(
        "rtnec,rtd->nrecd", dispatch, normed, preferred_element_type=jnp.float32
    ).astype(jnp.bfloat16)
    hidden = jnp.einsum(
        "srecd,edf->srecf",
        lax.all_to_all(outgoing, "req", split_axis=0, concat_axis=0, tiled=True),
        expert_gate_up,
        preferred_element_type=jnp.float32,
    )
    active = (jax.nn.silu(hidden[..., :FF]) * hidden[..., FF:]).astype(jnp.bfloat16)
    result = jnp.einsum(
        "srecf,efd->srecd", active, expert_down, preferred_element_type=jnp.float32
    ).astype(jnp.bfloat16)
    returned = lax.all_to_all(result, "req", split_axis=0, concat_axis=0, tiled=True)
    owner_of = route_flat // local_experts
    local_of = route_flat % local_experts
    flat_index = (
        (owner_of * req_rows + jnp.arange(req_rows)[:, None]) * local_experts + local_of
    ) * CAP + slot_index
    returned_rows = jnp.take(returned.reshape(-1, model_width), flat_index.reshape(-1), axis=0)
    returned_rows = returned_rows.reshape(req_rows, tok_rows, TOP, model_width)
    mixture = jnp.einsum(
        "rtk,rtkd->rtd",
        route_weights,
        returned_rows.astype(jnp.float32),
        precision=lax.Precision.HIGHEST,
    )
    return (attended_f + mixture).astype(jnp.bfloat16)


def layer_kernel(
    spans_ref,
    rec_ref,
    inverse_ref,
    q_ref,
    new_ref,
    cache_ref,
    held_ref,
    kw_ref,
    gain_ref,
    routes_ref,
    rw_ref,
    gu_hbm,
    dn_hbm,
    out_ref,
    gu_v,
    dn_v,
    kvsend,
    stsend,
    qsend,
    fsend,
    osend,
    crecv,
    srecv,
    qrecv,
    frecv,
    orecv,
    kbuf,
    vbuf,
    att,
    trecv,
    wrecv,
    total,
    psend,
    precv,
    load_sem,
    s_sem,
    r_sem,
    zs_sem,
    zr_sem,
    ts_sem,
    tr_sem,
):
    bf16 = jnp.bfloat16
    f32 = jnp.float32
    me = lax.axis_index("seq")
    S = lax.axis_size("seq")
    mz = lax.axis_index("req")
    N = lax.axis_size("req")
    groups = H // KVH
    tok = q_ref.shape[1]
    crows = cache_ref.shape[2]
    held = frecv.shape[0] // S
    width = q_ref.shape[2]
    local_experts = gu_v.shape[0]
    ctotal = S * crows
    stotal = S * tok

    barrier = pltpu.get_barrier_semaphore()
    for k in range(1, S):
        pl.semaphore_signal(barrier, inc=1, device_id={"seq": lax.rem(me + k, S)})
    for k in range(1, N):
        pl.semaphore_signal(barrier, inc=1, device_id={"req": lax.rem(mz + k, N)})

    def lanes(rows):
        return lax.broadcasted_iota(jnp.int32, (rows, 2 * HD), 1)

    def join(low, low_roll, high, high_roll, scale=None):
        a, b = low.astype(f32), high.astype(f32)
        a = pltpu.roll(a, HD, 1) if low_roll else a
        b = pltpu.roll(b, HD, 1) if high_roll else b
        c = jnp.where(lanes(a.shape[0]) < HD, a, b)
        return (c if scale is None else c * scale).astype(bf16)

    for h in range(KVH):
        cols = slice((h // 2) * 2 * HD, (h // 2 + 1) * 2 * HD)
        odd = h % 2 == 1
        for g in range(groups):
            c = h * groups + g
            qc = slice((c // 2) * 2 * HD, (c // 2 + 1) * 2 * HD)
            qsend[h, g] = join(q_ref[0, :, qc], c % 2 == 1, q_ref[1, :, qc], c % 2 == 0, HD**-0.5)
        for src, dst in ((cache_ref, kvsend), (new_ref, stsend)):
            dst[h, 0] = join(src[0, 0, :, cols], odd, src[1, 0, :, cols], not odd)
            dst[h, 1] = join(src[1, 1, :, cols], odd, src[0, 1, :, cols], not odd)

    def row_at(i, n):
        return pl.ds(pl.multiple_of(i * n, n), n)

    def exchange(kind, k, slot):
        peer = lax.rem(me + k, S)
        src, dst = (
            (qsend.at[peer], qrecv.at[:, row_at(slot, tok), :]),
            (stsend.at[peer], srecv.at[:, row_at(slot, tok), :]),
            (kvsend.at[peer, 0], crecv.at[0, row_at(slot, crows), :]),
            (kvsend.at[peer, 1], crecv.at[1, row_at(slot, crows), :]),
            (fsend.at[peer], frecv.at[row_at(slot, held), :]),
            (osend.at[:, row_at(peer, tok), :], orecv.at[slot]),
        )[kind]
        return pltpu.make_async_remote_copy(
            src_ref=src,
            dst_ref=dst,
            send_sem=s_sem.at[kind, k],
            recv_sem=r_sem.at[kind, k],
            device_id={"seq": peer},
        )

    def arrive(kind):
        for k in range(1, S):
            exchange(kind, k, lax.rem(me + S - k, S)).wait_recv()

    pl.semaphore_wait(barrier, S - 1 + N - 1)
    for k in range(1, S):
        for kind in (0, 1, 2):
            exchange(kind, k, me).start()

    loads = []
    for e in range(local_experts):
        loads.append(pltpu.make_async_copy(gu_hbm.at[e], gu_v.at[e], load_sem.at[0, e]))
        loads.append(pltpu.make_async_copy(dn_hbm.at[e], dn_v.at[e], load_sem.at[1, e]))

    fresh = jnp.dot(held_ref[...], kw_ref[...], preferred_element_type=f32)
    low_part = lax.broadcasted_iota(jnp.int32, fresh.shape, 1) % HD < HD // 2
    partner = jnp.where(
        low_part,
        pltpu.roll(fresh, fresh.shape[1] - HD // 2, 1),
        pltpu.roll(fresh, HD // 2, 1),
    )
    row_lane = lax.broadcasted_iota(jnp.int32, (held, S * held), 1)
    row_here = lax.broadcasted_iota(jnp.int32, (held, S * held), 0) + me * held
    positions = jnp.concatenate(
        [
            jnp.sum(
                jnp.where(row_lane == row_here, rec_ref[r : r + 1, :].astype(f32), 0.0),
                axis=1,
                keepdims=True,
            )
            for r in range(2)
        ],
        axis=0,
    )
    angles = positions * inverse_ref[...]
    cos_table, sin_table = jnp.cos(angles), jnp.sin(angles)
    sin_table = jnp.where(lanes(2 * held) % HD < HD // 2, -sin_table, sin_table)
    fresh = fresh * jnp.tile(cos_table, (1, KVH // 2)) + partner * jnp.tile(
        sin_table, (1, KVH // 2)
    )
    for h in range(KVH):
        cols = slice((h // 2) * 2 * HD, (h // 2 + 1) * 2 * HD)
        odd = h % 2 == 1
        fsend[h] = join(fresh[:held, cols], odd, fresh[held:, cols], not odd)
    for k in range(1, S):
        exchange(4, k, me).start()
    for k in range(1, S):
        exchange(3, k, me).start()
    for load in loads:
        load.start()

    qrecv[:, row_at(me, tok), :] = qsend[me]
    srecv[:, row_at(me, tok), :] = stsend[me]
    crecv[:, row_at(me, crows), :] = kvsend[me]
    frecv[row_at(me, held), :] = fsend[me]

    expert_row = lax.broadcasted_iota(jnp.int32, (128, tok), 0)
    for r in range(2):
        dense = jnp.zeros((128, tok), f32)
        for k in range(TOP):
            hit = routes_ref[r, k : k + 1, :] == expert_row
            dense = dense + jnp.where(hit, rw_ref[r, k : k + 1, :], 0.0)
        wrecv[mz, r * tok : (r + 1) * tok, :] = dense.T

    def share_copy(k, slot):
        return pltpu.make_async_remote_copy(
            src_ref=wrecv.at[mz],
            dst_ref=wrecv.at[slot],
            send_sem=zs_sem.at[0, k],
            recv_sem=zr_sem.at[0, k],
            device_id={"req": lax.rem(mz + k, N)},
        )

    def back_copy(r, k, slot):
        peer = lax.rem(mz + k, N)
        return pltpu.make_async_remote_copy(
            src_ref=psend.at[r, peer],
            dst_ref=precv.at[r, slot],
            send_sem=zs_sem.at[1 + r, k],
            recv_sem=zr_sem.at[1 + r, k],
            device_id={"req": peer},
        )

    def token_copy(r, origin, way):
        return pltpu.make_async_remote_copy(
            src_ref=trecv.at[r, origin],
            dst_ref=trecv.at[r, origin],
            send_sem=ts_sem.at[way, r, origin],
            recv_sem=tr_sem.at[r, origin],
            device_id={"req": mz + 1 if way == 0 else mz - 1},
        )

    def send_tokens(r, origin, way):
        @pl.when(mz < N - 1 if way == 0 else mz > 0)
        def _():
            token_copy(r, origin, way).start()

    def relay(d, r):
        @pl.when(mz - d >= 0)
        def _():
            token_copy(r, mz - d, 0).wait_recv()
            send_tokens(r, mz - d, 0)

        @pl.when(mz + d < N)
        def _():
            token_copy(r, mz + d, 1).wait_recv()
            send_tokens(r, mz + d, 1)

    for k in range(1, N):
        share_copy(k, mz).start()

    for kind in (0, 1, 2, 4):
        arrive(kind)
    for r in range(2):
        if r == 1:
            arrive(3)
        key_half = (lanes(crows) < HD) if r == 0 else (lanes(crows) >= HD)
        ones = jnp.ones((S * held, 2 * HD), bf16)
        spread = jnp.concatenate([frecv[...], ones], axis=1)
        wanted = rec_ref[r : r + 1, :]

        def place(i, carry):
            rows = row_at(i, crows)
            kv = crecv[r, rows, :].astype(f32)
            where_to = lax.broadcasted_iota(jnp.int32, (crows, S * held), 0) + i * crows
            hit = jnp.where(where_to == wanted, 1.0, 0.0).astype(bf16)
            both = jnp.dot(hit, spread, preferred_element_type=f32)
            keys = jnp.where(both[:, 2 * HD :] > 0.5, both[:, : 2 * HD], kv)
            kbuf[rows, :] = jnp.where(key_half, keys, 0.0).astype(bf16)
            vbuf[rows, :] = jnp.where(key_half, 1.0, kv).astype(bf16)
            return carry

        lax.fori_loop(0, S, place, 0)
        step = srecv[r].astype(f32)
        step_half = (lanes(stotal) < HD) if r == 0 else (lanes(stotal) >= HD)
        kbuf[ctotal:, :] = jnp.where(step_half, step, 0.0).astype(bf16)
        vbuf[ctotal:, :] = jnp.where(step_half, 1.0, step).astype(bf16)
        position = lax.broadcasted_iota(jnp.int32, (1, ctotal), 1)
        open_row = (position >= spans_ref[r, 0]) & (position < spans_ref[r, 1])
        bias = jnp.where(open_row, 0.0, NEG)
        causal = lax.broadcasted_iota(jnp.int32, (stotal, stotal), 1) <= lax.broadcasted_iota(
            jnp.int32, (stotal, stotal), 0
        )
        contract = (((1,), (1,)), ((), ()))

        def attend(g, carry):
            query = qrecv[g]
            old = lax.dot_general(
                query, kbuf[:ctotal, :], contract, preferred_element_type=f32
            ) + bias
            new = lax.dot_general(query, kbuf[ctotal:, :], contract, preferred_element_type=f32)
            new = jnp.where(causal, new, NEG)
            highest = jnp.maximum(
                jnp.max(old, axis=-1, keepdims=True), jnp.max(new, axis=-1, keepdims=True)
            )
            mixed = jnp.dot(
                jnp.exp(old - highest).astype(bf16), vbuf[:ctotal, :], preferred_element_type=f32
            ) + jnp.dot(
                jnp.exp(new - highest).astype(bf16), vbuf[ctotal:, :], preferred_element_type=f32
            )
            mixed = mixed / pltpu.roll(mixed, HD, 1)
            if r == 0:
                osend[g] = mixed.astype(bf16)
            else:
                osend[g] = jnp.where(
                    lanes(stotal) < HD, mixed, osend[g].astype(f32)
                ).astype(bf16)
            return carry

        lax.fori_loop(0, groups, attend, 0)

    for k in range(1, S):
        exchange(5, k, me).start()
    orecv[me] = osend[:, row_at(me, tok), :]
    arrive(5)
    for pair in range(H // 2):
        first, second = 2 * pair, 2 * pair + 1
        one = orecv[first // groups, first % groups]
        two = orecv[second // groups, second % groups]
        cols = slice(pair * 2 * HD, (pair + 1) * 2 * HD)
        att[:tok, cols] = join(one, True, two, False)
        att[tok:, cols] = join(one, False, two, True)
    attended = att[...].astype(f32)
    mean_square = jnp.mean(attended * attended, axis=-1, keepdims=True)
    normed = (attended * lax.rsqrt(mean_square + 1e-06) * gain_ref[...].reshape(1, width)).astype(bf16)
    for r in range(2):
        trecv[r, mz] = normed[r * tok : (r + 1) * tok]
        for way in range(2):
            send_tokens(r, mz, way)
    for k in range(1, N):
        share_copy(k, lax.rem(mz + N - k, N)).wait_recv()
    for load in loads:
        load.wait()
    for d in range(1, N - 1):
        for r in range(2):
            relay(d, r)
    rows_total = N * tok
    for r in range(2):
        relay(N - 1, r)
        total[...] = jnp.zeros_like(total)

        def expert(e, carry):
            tokens = trecv[r].reshape(rows_total, width)
            hidden = jnp.dot(tokens, gu_v[e], preferred_element_type=f32)
            gate, up = hidden[:, :FF], hidden[:, FF:]
            active = (gate / (1.0 + jnp.exp(-gate)) * up).astype(bf16)
            result = jnp.dot(active, dn_v[e], preferred_element_type=f32).astype(bf16)
            weights = wrecv[:, r * tok : (r + 1) * tok, :].reshape(rows_total, 128)
            lane = lax.broadcasted_iota(jnp.int32, weights.shape, 1)
            share = jnp.sum(
                jnp.where(lane == mz * local_experts + e, weights, 0.0), axis=1, keepdims=True
            )
            total[...] += result.astype(f32) * share
            return carry

        lax.fori_loop(0, local_experts, expert, 0)
        psend[r] = total[...].astype(bf16).reshape(N, tok, width)
        for k in sorted(range(1, N), key=lambda k: abs(2 * k - N)):
            back_copy(r, k, mz).start()
    for r in range(2):
        rows = slice(r * tok, (r + 1) * tok)
        mixture = att[rows, :].astype(f32) + psend[r, mz].astype(f32)
        for k in range(1, N):
            back_copy(r, k, lax.rem(mz + N - k, N)).wait_recv()
        for k in range(1, N):
            mixture = mixture + precv[r, lax.rem(mz + N - k, N)].astype(f32)
        out_ref[rows, :] = mixture.astype(bf16)
    for kind in range(6):
        for k in range(1, S):
            exchange(kind, k, me).wait_send()
    for k in range(1, N):
        share_copy(k, mz).wait_send()
        for r in range(2):
            back_copy(r, k, mz).wait_send()
    for r in range(2):
        for origin in range(N):

            @pl.when((origin <= mz) & (mz < N - 1))
            def _():
                token_copy(r, origin, 0).wait_send()

            @pl.when((origin >= mz) & (mz > 0))
            def _():
                token_copy(r, origin, 1).wait_send()


def head_parallel_body(
    queries,
    new_kv,
    cache_kv,
    cache_spans,
    recompute_rows,
    held_states,
    key_weight,
    norm_gain,
    routes,
    route_weights,
    expert_gate_up,
    expert_down,
):
    S = lax.axis_size("seq")
    N = lax.axis_size("req")
    req_rows, tok, width = queries.shape
    crows = cache_kv.shape[2]
    held = held_states.shape[1]
    local_experts = expert_gate_up.shape[0]
    groups = H // KVH
    bf16, f32 = jnp.bfloat16, jnp.float32
    half = HD // 2
    inverse = THETA ** (-((np.arange(2 * HD) % half) * (2.0 / HD)))
    inverse = jnp.asarray(inverse.astype(np.float32).reshape(1, 2 * HD))
    vmem = pl.BlockSpec(memory_space=pltpu.VMEM)
    smem = pl.BlockSpec(memory_space=pltpu.SMEM)
    hbm = pl.BlockSpec(memory_space=pl.ANY)
    lane = 2 * HD
    rows = req_rows * tok
    out = pl.pallas_call(
        layer_kernel,
        out_shape=pltpu.VMEM((rows, width), bf16),
        in_specs=[smem] + [vmem] * 10 + [hbm, hbm],
        out_specs=vmem,
        scratch_shapes=[
            pltpu.VMEM(expert_gate_up.shape, bf16),
            pltpu.VMEM(expert_down.shape, bf16),
            pltpu.VMEM((S, 2, crows, lane), bf16),
            pltpu.VMEM((S, 2, tok, lane), bf16),
            pltpu.VMEM((S, groups, tok, lane), bf16),
            pltpu.VMEM((S, held, lane), bf16),
            pltpu.VMEM((groups, S * tok, lane), bf16),
            pltpu.VMEM((2, S * crows, lane), bf16),
            pltpu.VMEM((2, S * tok, lane), bf16),
            pltpu.VMEM((groups, S * tok, lane), bf16),
            pltpu.VMEM((S * held, lane), bf16),
            pltpu.VMEM((S, groups, tok, lane), bf16),
            pltpu.VMEM((S * (crows + tok), lane), bf16),
            pltpu.VMEM((S * (crows + tok), lane), bf16),
            pltpu.VMEM((rows, width), bf16),
            pltpu.VMEM((2, N, tok, width), bf16),
            pltpu.VMEM((N, rows, 128), f32),
            pltpu.VMEM((N * tok, width), f32),
            pltpu.VMEM((2, N, tok, width), bf16),
            pltpu.VMEM((2, N, tok, width), bf16),
            pltpu.SemaphoreType.DMA((2, local_experts)),
            pltpu.SemaphoreType.DMA((6, S)),
            pltpu.SemaphoreType.DMA((6, S)),
            pltpu.SemaphoreType.DMA((3, N)),
            pltpu.SemaphoreType.DMA((3, N)),
            pltpu.SemaphoreType.DMA((2, 2, N)),
            pltpu.SemaphoreType.DMA((2, N)),
        ],
        compiler_params=pltpu.CompilerParams(
            collective_id=0, has_side_effects=True, vmem_limit_bytes=60 << 20
        ),
        name="layer",
    )(
        cache_spans,
        recompute_rows,
        inverse,
        queries,
        new_kv,
        cache_kv,
        held_states.reshape(req_rows * held, width),
        key_weight,
        norm_gain,
        jnp.transpose(routes, (0, 2, 1)),
        jnp.transpose(route_weights, (0, 2, 1)),
        expert_gate_up,
        expert_down,
    )
    return out.reshape(req_rows, tok, width)


def solution(mesh):
    body = head_parallel_body if mesh.shape["seq"] == KVH else body_wide
    in_specs = (
        P("req", "seq", None),
        P(None, "req", "seq", None),
        P(None, "req", "seq", None),
        P("req", None),
        P("req", None),
        P("req", "seq", None),
        P(),
        P(),
        P("req", "seq", None),
        P("req", "seq", None),
        P("req", None, None),
        P("req", None, None),
    )
    out_specs = P("req", "seq", None)
    return jax.shard_map(body, mesh=mesh, in_specs=in_specs, out_specs=out_specs, check_vma=False)
```

```python
import jax
import jax.numpy as jnp
import numpy as np
from jax import lax
from jax.experimental import pallas as pl
from jax.experimental.pallas import tpu as pltpu
from jax.sharding import PartitionSpec as P

H = 24
KVH = 8
HD = 64
FF = 512
TOP = 8
CAP = 16


NEG = -1e30
THETA = 10000.0


def rotate(key_heads, positions):
    half_dim = key_heads.shape[-1] // 2
    exponent = jnp.arange(half_dim).astype(jnp.float32) * (2.0 / key_heads.shape[-1])
    inverse = THETA ** (-exponent)
    angles = positions.astype(jnp.float32)[..., None] * inverse
    cosine = jnp.cos(angles)[..., None, :]
    sine_part = jnp.sin(angles)[..., None, :]
    lower_half = key_heads[..., :half_dim]
    upper_half = key_heads[..., half_dim:]
    return jnp.concatenate(
        [
            lower_half * cosine - upper_half * sine_part,
            upper_half * cosine + lower_half * sine_part,
        ],
        axis=-1,
    )


def partial_attend(packed):
    query_rows, key_rows, value_rows, allowed = packed
    query_count, model_width = query_rows.shape
    key_count = key_rows.shape[0]
    groups = H // KVH
    query_heads = query_rows.reshape(query_count, KVH, groups, HD)
    key_heads = key_rows.reshape(key_count, KVH, HD)
    value_heads = value_rows.reshape(key_count, KVH, HD)
    scores = jnp.einsum(
        "qkgd,nkd->kgqn", query_heads, key_heads, preferred_element_type=jnp.float32
    ) * HD ** (-0.5)
    scores = jnp.where(allowed[None, None, :, :], scores, NEG)
    highest = jnp.max(scores, axis=-1, keepdims=True)
    exps = jnp.exp(scores - highest)
    totals = jnp.sum(exps, axis=-1)
    weights = exps.astype(jnp.bfloat16)
    mixed_rows = jnp.einsum(
        "kgqn,nkd->qkgd", weights, value_heads, preferred_element_type=jnp.float32
    )
    mixed_rows = mixed_rows / jnp.transpose(totals, (2, 0, 1))[..., None]
    log_total = highest[..., 0] + jnp.log(totals)
    log_rows = jnp.transpose(log_total, (2, 0, 1)).reshape(query_count, H)
    return (mixed_rows.reshape(query_count, model_width), log_rows)


def body_wide(
    queries,
    new_kv,
    cache_kv,
    cache_spans,
    recompute_rows,
    held_states,
    key_weight,
    norm_gain,
    routes,
    route_weights,
    expert_gate_up,
    expert_down,
):
    seq_index = lax.axis_index("seq")
    seq_count = lax.axis_size("seq")
    owner_count = lax.axis_size("req")
    req_rows, tok_rows, model_width = queries.shape
    cache_rows = cache_kv.shape[2]
    held_rows = held_states.shape[1]
    local_experts = expert_gate_up.shape[0]
    expert_total = owner_count * local_experts
    my_positions = lax.dynamic_slice_in_dim(recompute_rows, seq_index * held_rows, held_rows, 1)
    projected = jnp.dot(
        held_states.reshape(req_rows * held_rows, model_width),
        key_weight,
        preferred_element_type=jnp.float32,
    )
    rotated = rotate(projected.reshape(req_rows, held_rows, KVH, HD), my_positions)
    rotated = rotated.reshape(req_rows, held_rows, KVH * HD).astype(jnp.bfloat16)
    fresh_rows = lax.all_gather(rotated, "seq", axis=1, tiled=True)
    cache_positions = seq_index * cache_rows + jnp.arange(cache_rows)
    hit_table = recompute_rows[:, None, :] == cache_positions[None, :, None]
    placed = jnp.einsum(
        "rcm,rmk->rck",
        hit_table.astype(jnp.bfloat16),
        fresh_rows,
        preferred_element_type=jnp.float32,
    ).astype(jnp.bfloat16)
    cache_keys = jnp.where(jnp.any(hit_table, axis=2)[:, :, None], placed, cache_kv[0])
    span_start = cache_spans[:, 0:1]
    span_end = cache_spans[:, 1:2]
    all_queries = lax.all_gather(queries, "seq", axis=1, tiled=True)
    step_total = all_queries.shape[1]
    cache_allowed = (cache_positions[None, :] >= span_start) & (cache_positions[None, :] < span_end)
    key_positions = seq_index * tok_rows + jnp.arange(tok_rows)
    step_allowed = key_positions[None, :] <= jnp.arange(step_total)[:, None]
    allowed = jnp.concatenate(
        [
            jnp.broadcast_to(cache_allowed[:, None, :], (req_rows, step_total, cache_rows)),
            jnp.broadcast_to(step_allowed[None], (req_rows, step_total, tok_rows)),
        ],
        axis=2,
    )
    key_rows = jnp.concatenate([cache_keys, new_kv[0]], axis=1)
    value_rows = jnp.concatenate([cache_kv[1], new_kv[1]], axis=1)
    part_out, part_log = lax.map(partial_attend, (all_queries, key_rows, value_rows, allowed))
    piece_out, piece_log = (
        lax.all_to_all(part_out[None], "seq", split_axis=2, concat_axis=0, tiled=True),
        lax.all_to_all(part_log[None], "seq", split_axis=2, concat_axis=0, tiled=True),
    )
    best_log = jnp.max(piece_log, axis=0)
    factors = jnp.exp(piece_log - best_log[None])
    factor_sum = jnp.sum(factors, axis=0)
    spread_out = piece_out.reshape(seq_count, req_rows, tok_rows, H, HD)
    combined = jnp.sum(spread_out * factors[..., None], axis=0) / factor_sum[..., None]
    attended_f = combined.reshape(req_rows, tok_rows, model_width)
    attended = attended_f.astype(jnp.bfloat16)
    attended_f = attended.astype(jnp.float32)
    mean_square = jnp.mean(attended_f * attended_f, axis=-1, keepdims=True)
    normed = (attended_f * lax.rsqrt(mean_square + 1e-06) * norm_gain).astype(jnp.bfloat16)
    route_flat = routes.reshape(req_rows, tok_rows * TOP)
    expert_match = (route_flat[:, :, None] == jnp.arange(expert_total)[None, None, :]).astype(
        jnp.int32
    )
    order = jnp.arange(tok_rows * TOP)
    before = (order[None, :] < order[:, None]).astype(jnp.bfloat16)
    earlier = jnp.einsum(
        "ij,rje->rie",
        before,
        expert_match.astype(jnp.bfloat16),
        preferred_element_type=jnp.float32,
    ).astype(jnp.int32)
    slot_index = jnp.sum(earlier * expert_match, axis=2)
    target = route_flat * CAP + slot_index
    slot_match = target[:, :, None] == jnp.arange(expert_total * CAP)[None, None, :]
    dispatch = jnp.any(
        slot_match.reshape(req_rows, tok_rows, TOP, expert_total * CAP), axis=2
    ).astype(jnp.bfloat16)
    dispatch = dispatch.reshape(req_rows, tok_rows, owner_count, local_experts, CAP)
    outgoing = jnp.einsum(
        "rtnec,rtd->nrecd", dispatch, normed, preferred_element_type=jnp.float32
    ).astype(jnp.bfloat16)
    hidden = jnp.einsum(
        "srecd,edf->srecf",
        lax.all_to_all(outgoing, "req", split_axis=0, concat_axis=0, tiled=True),
        expert_gate_up,
        preferred_element_type=jnp.float32,
    )
    active = (jax.nn.silu(hidden[..., :FF]) * hidden[..., FF:]).astype(jnp.bfloat16)
    result = jnp.einsum(
        "srecf,efd->srecd", active, expert_down, preferred_element_type=jnp.float32
    ).astype(jnp.bfloat16)
    returned = lax.all_to_all(result, "req", split_axis=0, concat_axis=0, tiled=True)
    owner_of = route_flat // local_experts
    local_of = route_flat % local_experts
    flat_index = (
        (owner_of * req_rows + jnp.arange(req_rows)[:, None]) * local_experts + local_of
    ) * CAP + slot_index
    returned_rows = jnp.take(returned.reshape(-1, model_width), flat_index.reshape(-1), axis=0)
    returned_rows = returned_rows.reshape(req_rows, tok_rows, TOP, model_width)
    mixture = jnp.einsum(
        "rtk,rtkd->rtd",
        route_weights,
        returned_rows.astype(jnp.float32),
        precision=lax.Precision.HIGHEST,
    )
    return (attended_f + mixture).astype(jnp.bfloat16)


def layer_kernel(
    spans_ref,
    rec_ref,
    inverse_ref,
    gain_ref,
    routes_ref,
    rw_ref,
    q_hbm,
    new_hbm,
    cache_hbm,
    held_hbm,
    kw_hbm,
    gu_hbm,
    dn_hbm,
    out_ref,
    q_in,
    new_in,
    cache_in,
    held_in,
    kw_in,
    gu_v,
    dn_v,
    kvsend,
    stsend,
    qsend,
    fsend,
    osend,
    crecv,
    srecv,
    qrecv,
    frecv,
    orecv,
    placed,
    keep,
    att,
    trecv,
    wrecv,
    act,
    total,
    psend,
    precv,
    in_sem,
    load_sem,
    s_sem,
    r_sem,
    zs_sem,
    zr_sem,
    ts_sem,
    tr_sem,
):
    bf16 = jnp.bfloat16
    f32 = jnp.float32
    me = lax.axis_index("seq")
    S = lax.axis_size("seq")
    mz = lax.axis_index("req")
    N = lax.axis_size("req")
    groups = H // KVH
    tok = q_in.shape[1]
    crows = cache_in.shape[2]
    held = frecv.shape[0] // S
    width = q_in.shape[2]
    local_experts = gu_v.shape[0]
    stotal = S * tok
    lane = 2 * HD
    Q, NEW, FRESH, KV, OUT = 0, 1, 2, 3, 5
    near = mz + 1 - 2 * lax.rem(mz, 2)
    across = mz + 2 - 4 * (mz // 2)
    mirror = N - 1 - mz
    other = (mz, near, across, mirror)
    inner = (mz == 1) | (mz == 2)

    barrier = pltpu.get_barrier_semaphore()
    for k in range(1, S):
        pl.semaphore_signal(barrier, inc=1, device_id={"seq": lax.rem(me + k, S)})
    for k in range(1, N):
        pl.semaphore_signal(barrier, inc=1, device_id={"req": lax.rem(mz + k, N)})

    inputs = [
        pltpu.make_async_copy(src, dst, in_sem.at[i])
        for i, (src, dst) in enumerate(
            (
                (q_hbm, q_in),
                (new_hbm, new_in),
                (held_hbm, held_in),
                (kw_hbm, kw_in),
                (cache_hbm.at[:, 0], cache_in.at[0]),
                (cache_hbm.at[:, 1], cache_in.at[1]),
            )
        )
    ]
    for copy in inputs:
        copy.start()

    def lanes(rows):
        return lax.broadcasted_iota(jnp.int32, (rows, lane), 1)

    def swap(x):
        return pltpu.roll(x, HD, 1)

    def merge(low, high):
        return jnp.where(lanes(low.shape[0]) < HD, low, high)

    def join(low, low_roll, high, high_roll, scale=None):
        a, b = low.astype(f32), high.astype(f32)
        a = swap(a) if low_roll else a
        b = swap(b) if high_roll else b
        c = merge(a, b)
        return (c if scale is None else c * scale).astype(bf16)

    def pair_cols(h):
        return slice((h // 2) * lane, (h // 2 + 1) * lane), h % 2 == 1

    def row_at(i, n):
        return pl.ds(pl.multiple_of(i * n, n), n)

    def exchange(kind, k, slot):
        peer = lax.rem(me + k, S)
        src, dst = (
            (qsend.at[peer], qrecv.at[:, row_at(slot, tok), :]),
            (stsend.at[peer], srecv.at[:, row_at(slot, tok), :]),
            (fsend.at[peer], frecv.at[row_at(slot, held), :]),
            (kvsend.at[0, peer], crecv.at[0, slot]),
            (kvsend.at[1, peer], crecv.at[1, slot]),
            (osend.at[0, peer], orecv.at[0, slot]),
            (osend.at[1, peer], orecv.at[1, slot]),
        )[kind]
        return pltpu.make_async_remote_copy(
            src_ref=src,
            dst_ref=dst,
            send_sem=s_sem.at[kind, k],
            recv_sem=r_sem.at[kind, k],
            device_id={"seq": peer},
        )

    def send(kind, steps=None):
        for k in range(1, S) if steps is None else steps:
            exchange(kind, k, me).start()

    def arrive_from(kind, k):
        exchange(kind, k, lax.rem(me + S - k, S)).wait_recv()

    def arrive(kind):
        for k in range(1, S):
            arrive_from(kind, k)

    inputs[0].wait()
    inputs[1].wait()
    for h in range(KVH):
        cols, odd = pair_cols(h)
        for g in range(groups):
            c = h * groups + g
            qc, _ = pair_cols(c)
            qsend[h, g] = join(q_in[0, :, qc], c % 2 == 1, q_in[1, :, qc], c % 2 == 0, HD**-0.5)
        stsend[h, 0] = join(new_in[0, 0, :, cols], odd, new_in[1, 0, :, cols], not odd)
        stsend[h, 1] = join(new_in[1, 1, :, cols], odd, new_in[0, 1, :, cols], not odd)

    pl.semaphore_wait(barrier, S - 1 + N - 1)
    send(Q)
    send(NEW)

    def pack_cache(r):
        inputs[4 + r].wait()
        for h in range(KVH):
            cols, odd = pair_cols(h)
            keys, values = cache_in[r, 0, :, cols], cache_in[r, 1, :, cols]
            low, high = (keys, values) if r == 0 else (values, keys)
            kvsend[r, h] = join(low, odd, high, not odd)

    pack_cache(0)
    send(KV, (1, 2))

    inputs[2].wait()
    inputs[3].wait()
    fresh = jnp.dot(held_in[...], kw_in[...], preferred_element_type=f32)
    low_part = lax.broadcasted_iota(jnp.int32, fresh.shape, 1) % HD < HD // 2
    partner = jnp.where(
        low_part,
        pltpu.roll(fresh, fresh.shape[1] - HD // 2, 1),
        pltpu.roll(fresh, HD // 2, 1),
    )
    row_lane = lax.broadcasted_iota(jnp.int32, (held, S * held), 1)
    row_here = lax.broadcasted_iota(jnp.int32, (held, S * held), 0) + me * held
    positions = jnp.concatenate(
        [
            jnp.sum(
                jnp.where(row_lane == row_here, rec_ref[r : r + 1, :].astype(f32), 0.0),
                axis=1,
                keepdims=True,
            )
            for r in range(2)
        ],
        axis=0,
    )
    angles = positions * inverse_ref[...]
    cos_table, sin_table = jnp.cos(angles), jnp.sin(angles)
    sin_table = jnp.where(lanes(2 * held) % HD < HD // 2, -sin_table, sin_table)
    fresh = fresh * jnp.tile(cos_table, (1, KVH // 2)) + partner * jnp.tile(
        sin_table, (1, KVH // 2)
    )
    for h in range(KVH):
        cols, odd = pair_cols(h)
        fsend[h] = join(fresh[:held, cols], odd, fresh[held:, cols], not odd)
    send(FRESH)
    send(KV, range(3, S))

    loads = []
    for e in range(local_experts):
        loads.append(pltpu.make_async_copy(gu_hbm.at[e], gu_v.at[e], load_sem.at[0, e]))
    for e in range(local_experts):
        loads.append(pltpu.make_async_copy(dn_hbm.at[e], dn_v.at[e], load_sem.at[1, e]))
    for load in loads:
        load.start()

    pack_cache(1)

    expert_row = lax.broadcasted_iota(jnp.int32, (128, tok), 0)
    for r in range(2):
        dense = jnp.zeros((128, tok), f32)
        for k in range(TOP):
            hit = routes_ref[r, k : k + 1, :] == expert_row
            dense = dense + jnp.where(hit, rw_ref[r, k : k + 1, :], 0.0)
        wrecv[mz, r * tok : (r + 1) * tok, :] = dense.T

    def share_copy(k, slot):
        return pltpu.make_async_remote_copy(
            src_ref=wrecv.at[mz],
            dst_ref=wrecv.at[slot],
            send_sem=zs_sem.at[0, k],
            recv_sem=zr_sem.at[0, k],
            device_id={"req": lax.rem(mz + k, N)},
        )

    def back_copy(r, half, block, to, slot):
        return pltpu.make_async_remote_copy(
            src_ref=psend.at[r, half, other[block]],
            dst_ref=precv.at[r, half, slot],
            send_sem=zs_sem.at[1 + 2 * r + half, block],
            recv_sem=zr_sem.at[1 + 2 * r + half, slot],
            device_id={"req": other[to]},
        )

    def token_copy(r, origin, to, way):
        return pltpu.make_async_remote_copy(
            src_ref=trecv.at[r, origin],
            dst_ref=trecv.at[r, origin],
            send_sem=ts_sem.at[r, way],
            recv_sem=tr_sem.at[r, origin],
            device_id={"req": other[to]},
        )

    def send_tokens(r):
        token_copy(r, mz, 2, 2).start()

        @pl.when(inner)
        def _():
            token_copy(r, mz, 3, 3).start()

        token_copy(r, mz, 1, 1).start()

    def relay_tokens(r):
        token_copy(r, across, 1, 0).wait_recv()

        @pl.when(inner)
        def _():
            token_copy(r, across, 1, 0).start()

    def rest_of_tokens(r):
        token_copy(r, near, 1, 0).wait_recv()
        token_copy(r, mirror, 1, 0).wait_recv()

    def send_back(r, half):
        @pl.when(inner)
        def _():
            back_copy(r, half, 3, 3, 3).start()

        @pl.when(jnp.logical_not(inner))
        def _():
            back_copy(r, half, 3, 1, 0).start()
            back_copy(r, half, 2, 2, 2).start()

        back_copy(r, half, 1, 1, 1).start()

    def relay_back(r, half):
        @pl.when(inner)
        def _():
            back_copy(r, half, 3, 1, 0).wait_recv()
            both = psend[r, half, across].astype(f32) + precv[r, half, 0].astype(f32)
            psend[r, half, across] = both.astype(bf16)
            back_copy(r, half, 2, 2, 2).start()

    for k in range(1, N):
        share_copy(k, mz).start()

    qrecv[:, row_at(me, tok), :] = qsend[me]
    srecv[:, row_at(me, tok), :] = stsend[me]
    frecv[row_at(me, held), :] = fsend[me]
    arrive(Q)
    arrive(NEW)
    arrive(FRESH)
    ones = jnp.ones((S * held, lane), bf16)
    spread = jnp.concatenate([frecv[...], ones], axis=1)
    for r in range(2):
        wanted = rec_ref[r : r + 1, :]

        def place(i, carry):
            where_to = lax.broadcasted_iota(jnp.int32, (crows, S * held), 0) + i * crows
            hit = jnp.where(where_to == wanted, 1.0, 0.0).astype(bf16)
            both = jnp.dot(hit, spread, preferred_element_type=f32)
            placed[r, i] = both[:, :lane].astype(bf16)
            keep[r, i] = (1.0 - both[:, lane:]).astype(bf16)
            return carry

        lax.fori_loop(0, S, place, 0)

    for k in range(1, S):
        exchange(KV, k, me).wait_send()
    early = range(1, 5)
    late = range(5, S)
    send(KV + 1, early)

    contract = (((1,), (1,)), ((), ()))

    def key_lanes(r, rows):
        return lanes(rows) < HD if r == 0 else lanes(rows) >= HD

    def chunk(r, state, query, keys, raw, bias=None, mask=None):
        scores = lax.dot_general(query, keys, contract, preferred_element_type=f32)
        if bias is not None:
            scores = scores + bias
        if mask is not None:
            scores = jnp.where(mask, scores, NEG)
        values = jnp.where(key_lanes(r, raw.shape[0]), jnp.ones_like(raw), raw)
        highest = jnp.max(scores, axis=-1, keepdims=True)
        if state is None:
            exps = jnp.exp(scores - highest).astype(bf16)
            return highest, jnp.dot(exps, values, preferred_element_type=f32)
        before, mixed = state
        highest = jnp.maximum(before, highest)
        exps = jnp.exp(scores - highest).astype(bf16)
        mixed = mixed * jnp.exp(before - highest)
        return highest, mixed + jnp.dot(exps, values, preferred_element_type=f32)

    def query_of(r):
        query = qrecv[...].reshape(groups * stotal, lane)
        return jnp.where(key_lanes(r, groups * stotal), query, jnp.zeros_like(query))

    def attend_new(r, query):
        rows = lax.broadcasted_iota(jnp.int32, (groups * stotal, stotal), 0) % stotal
        causal = lax.broadcasted_iota(jnp.int32, (groups * stotal, stotal), 1) <= rows
        return chunk(r, None, query, srecv[r], srecv[r], mask=causal)

    def attend_cache(r, state, query, k):
        source = lax.rem(me + S - k, S)
        raw = kvsend[r, source] if k == 0 else crecv[r, source]
        keys = placed[r, source] + keep[r, source] * raw
        position = lax.broadcasted_iota(jnp.int32, (1, crows), 1) + source * crows
        open_row = (position >= spans_ref[r, 0]) & (position < spans_ref[r, 1])
        return chunk(r, state, query, keys, raw, bias=jnp.where(open_row, 0.0, NEG))

    def finish(r, state):
        mixed = state[1]
        mixed = mixed / swap(mixed)
        turned = swap(mixed)
        low, high = (turned, mixed) if r == 0 else (mixed, turned)
        head = [slice(g * stotal, (g + 1) * stotal) for g in range(groups)]
        two = merge(low[head[0]], high[head[1]]).astype(bf16)
        osend[r, :, :tok, :] = two.reshape(S, tok, lane)
        half = tok // 2
        one_low = low[head[2]].reshape(S, tok, lane)[:, :half].reshape(S * half, lane)
        one_high = high[head[2]].reshape(S, tok, lane)[:, half:].reshape(S * half, lane)
        osend[r, :, tok:, :] = merge(one_low, one_high).astype(bf16).reshape(S, half, lane)
        send(OUT + r)
        orecv[r, me] = osend[r, me]

    def gather_heads(r):
        arrive(OUT + r)
        for p in range(S // 2):
            even, odd = orecv[r, 2 * p].astype(f32), orecv[r, 2 * p + 1].astype(f32)
            even_solo, odd_solo = even[tok:], odd[tok:]
            odd_two = swap(odd[:tok])
            tile_b = merge(jnp.concatenate([even_solo, swap(even_solo)], axis=0), odd_two)
            tile_c = merge(odd_two, jnp.concatenate([swap(odd_solo), odd_solo], axis=0))
            att[r, :, p * 3 * lane : (p + 1) * 3 * lane] = jnp.concatenate(
                [even[:tok], tile_b, tile_c], axis=1
            )
        attended = att[r]
        mean_square = jnp.mean(attended * attended, axis=-1, keepdims=True)
        gain = gain_ref[...].reshape(1, width)
        trecv[r, mz] = (attended * lax.rsqrt(mean_square + 1e-06) * gain).astype(bf16)
        send_tokens(r)

    query = query_of(0)
    state = attend_new(0, query)
    state = attend_cache(0, state, query, 0)
    for part in ((1, 2, 3), (4, 5), (6, 7)):
        for k in part:
            arrive_from(KV, k)
        for k in part:
            state = attend_cache(0, state, query, k)
    finish(0, state)
    send(KV + 1, late)

    query = query_of(1)
    state = attend_new(1, query)
    state = attend_cache(1, state, query, 0)
    for part in ((1, 2), (3, 4), (5, 6, 7)):
        for k in part:
            arrive_from(KV + 1, k)
        for k in part:
            state = attend_cache(1, state, query, k)
        if part[0] == 1:
            gather_heads(0)
    finish(1, state)
    relay_tokens(0)
    gather_heads(1)
    rest_of_tokens(0)
    for k in range(1, N):
        share_copy(k, lax.rem(mz + N - k, N)).wait_recv()

    rows_total = N * tok
    part_width = width // 2

    def experts(r):
        tokens = trecv[r].reshape(rows_total, width)
        weights = wrecv[:, r * tok : (r + 1) * tok, :].reshape(rows_total, 128)
        column = lax.broadcasted_iota(jnp.int32, weights.shape, 1)
        for e in range(local_experts):
            if r == 0:
                loads[e].wait()
            hidden = jnp.dot(tokens, gu_v[e], preferred_element_type=f32)
            gate, up = hidden[:, :FF], hidden[:, FF:]
            share = jnp.sum(
                jnp.where(column == mz * local_experts + e, weights, 0.0), axis=1, keepdims=True
            )
            act[:, e * FF : (e + 1) * FF] = (gate / (1.0 + jnp.exp(-gate)) * up * share).astype(
                bf16
            )
        if r == 0:
            for load in loads[local_experts:]:
                load.wait()
        down = dn_v[...].reshape(local_experts * FF, width)
        for half in range(2):
            summed = jnp.dot(
                act[...],
                down[:, half * part_width : (half + 1) * part_width],
                preferred_element_type=f32,
            )
            psend[r, half] = summed.astype(bf16).reshape(N, tok, part_width)
            send_back(r, half)

    experts(0)
    relay_tokens(1)
    for half in range(2):
        relay_back(0, half)
    rest_of_tokens(1)
    experts(1)
    for half in range(2):
        relay_back(1, half)
    for r in range(2):
        for half in range(2):
            cols = slice(half * part_width, (half + 1) * part_width)
            back_copy(r, half, 1, 1, 1).wait_recv()
            back_copy(r, half, 2, 2, 2).wait_recv()
            mixture = att[r, :, cols] + psend[r, half, mz].astype(f32)
            mixture = mixture + precv[r, half, 1].astype(f32) + precv[r, half, 2].astype(f32)
            total[r, :, cols] = mixture

            @pl.when(inner)
            def _():
                back_copy(r, half, 3, 3, 3).wait_recv()
                total[r, :, cols] += precv[r, half, 3].astype(f32)

            out_ref[r * tok : (r + 1) * tok, cols] = total[r, :, cols].astype(bf16)
    for kind in (Q, NEW, FRESH, KV + 1, OUT, OUT + 1):
        for k in range(1, S):
            exchange(kind, k, me).wait_send()
    for k in range(1, N):
        share_copy(k, mz).wait_send()
    for r in range(2):
        for half in range(2):
            for block in (1, 2, 3):
                back_copy(r, half, block, 1, 1).wait_send()
        for way in (1, 2):
            token_copy(r, mz, 1, way).wait_send()

        @pl.when(inner)
        def _():
            token_copy(r, mz, 3, 3).wait_send()
            token_copy(r, across, 1, 0).wait_send()


def head_parallel_body(
    queries,
    new_kv,
    cache_kv,
    cache_spans,
    recompute_rows,
    held_states,
    key_weight,
    norm_gain,
    routes,
    route_weights,
    expert_gate_up,
    expert_down,
):
    S = lax.axis_size("seq")
    N = lax.axis_size("req")
    req_rows, tok, width = queries.shape
    crows = cache_kv.shape[2]
    held = held_states.shape[1]
    local_experts = expert_gate_up.shape[0]
    groups = H // KVH
    bf16, f32 = jnp.bfloat16, jnp.float32
    half = HD // 2
    inverse = THETA ** (-((np.arange(2 * HD) % half) * (2.0 / HD)))
    inverse = jnp.asarray(inverse.astype(np.float32).reshape(1, 2 * HD))
    vmem = pl.BlockSpec(memory_space=pltpu.VMEM)
    smem = pl.BlockSpec(memory_space=pltpu.SMEM)
    hbm = pl.BlockSpec(memory_space=pl.ANY)
    lane = 2 * HD
    rows = req_rows * tok
    out = pl.pallas_call(
        layer_kernel,
        out_shape=pltpu.VMEM((rows, width), bf16),
        in_specs=[smem] + [vmem] * 5 + [hbm] * 7,
        out_specs=vmem,
        scratch_shapes=[
            pltpu.VMEM((req_rows, tok, width), bf16),
            pltpu.VMEM((2, req_rows, tok, KVH * HD), bf16),
            pltpu.VMEM((req_rows, 2, crows, KVH * HD), bf16),
            pltpu.VMEM((req_rows * held, width), bf16),
            pltpu.VMEM(key_weight.shape, bf16),
            pltpu.VMEM(expert_gate_up.shape, bf16),
            pltpu.VMEM(expert_down.shape, bf16),
            pltpu.VMEM((2, S, crows, lane), bf16),
            pltpu.VMEM((S, 2, tok, lane), bf16),
            pltpu.VMEM((S, groups, tok, lane), bf16),
            pltpu.VMEM((S, held, lane), bf16),
            pltpu.VMEM((2, S, tok * 3 // 2, lane), bf16),
            pltpu.VMEM((2, S, crows, lane), bf16),
            pltpu.VMEM((2, S * tok, lane), bf16),
            pltpu.VMEM((groups, S * tok, lane), bf16),
            pltpu.VMEM((S * held, lane), bf16),
            pltpu.VMEM((2, S, tok * 3 // 2, lane), bf16),
            pltpu.VMEM((2, S, crows, lane), bf16),
            pltpu.VMEM((2, S, crows, lane), bf16),
            pltpu.VMEM((2, tok, width), f32),
            pltpu.VMEM((2, N, tok, width), bf16),
            pltpu.VMEM((N, rows, 128), f32),
            pltpu.VMEM((N * tok, local_experts * FF), bf16),
            pltpu.VMEM((2, tok, width), f32),
            pltpu.VMEM((2, 2, N, tok, width // 2), bf16),
            pltpu.VMEM((2, 2, N, tok, width // 2), bf16),
            pltpu.SemaphoreType.DMA((6,)),
            pltpu.SemaphoreType.DMA((2, local_experts)),
            pltpu.SemaphoreType.DMA((7, S)),
            pltpu.SemaphoreType.DMA((7, S)),
            pltpu.SemaphoreType.DMA((5, N)),
            pltpu.SemaphoreType.DMA((5, N)),
            pltpu.SemaphoreType.DMA((2, N)),
            pltpu.SemaphoreType.DMA((2, N)),
        ],
        compiler_params=pltpu.CompilerParams(
            collective_id=0, has_side_effects=True, vmem_limit_bytes=60 << 20
        ),
        name="layer",
    )(
        cache_spans,
        recompute_rows,
        inverse,
        norm_gain,
        jnp.transpose(routes, (0, 2, 1)),
        jnp.transpose(route_weights, (0, 2, 1)),
        queries,
        new_kv,
        cache_kv,
        held_states.reshape(req_rows * held, width),
        key_weight,
        expert_gate_up,
        expert_down,
    )
    return out.reshape(req_rows, tok, width)


def solution(mesh):
    by_heads = mesh.shape["seq"] == KVH and mesh.shape["req"] == 4
    body = head_parallel_body if by_heads else body_wide
    in_specs = (
        P("req", "seq", None),
        P(None, "req", "seq", None),
        P(None, "req", "seq", None),
        P("req", None),
        P("req", None),
        P("req", "seq", None),
        P(),
        P(),
        P("req", "seq", None),
        P("req", "seq", None),
        P("req", None, None),
        P("req", None, None),
    )
    out_specs = P("req", "seq", None)
    return jax.shard_map(body, mesh=mesh, in_specs=in_specs, out_specs=out_specs, check_vma=False)
```

```python
import jax
import jax.numpy as jnp
import numpy as np
from jax import lax
from jax.experimental import pallas as pl
from jax.experimental.pallas import tpu as pltpu
from jax.sharding import PartitionSpec as P

H = 24
KVH = 8
HD = 64
FF = 512
TOP = 8
CAP = 16


NEG = -1e30
THETA = 10000.0


def rotate(key_heads, positions):
    half_dim = key_heads.shape[-1] // 2
    exponent = jnp.arange(half_dim).astype(jnp.float32) * (2.0 / key_heads.shape[-1])
    inverse = THETA ** (-exponent)
    angles = positions.astype(jnp.float32)[..., None] * inverse
    cosine = jnp.cos(angles)[..., None, :]
    sine_part = jnp.sin(angles)[..., None, :]
    lower_half = key_heads[..., :half_dim]
    upper_half = key_heads[..., half_dim:]
    return jnp.concatenate(
        [
            lower_half * cosine - upper_half * sine_part,
            upper_half * cosine + lower_half * sine_part,
        ],
        axis=-1,
    )


def partial_attend(packed):
    query_rows, key_rows, value_rows, allowed = packed
    query_count, model_width = query_rows.shape
    key_count = key_rows.shape[0]
    groups = H // KVH
    query_heads = query_rows.reshape(query_count, KVH, groups, HD)
    key_heads = key_rows.reshape(key_count, KVH, HD)
    value_heads = value_rows.reshape(key_count, KVH, HD)
    scores = jnp.einsum(
        "qkgd,nkd->kgqn", query_heads, key_heads, preferred_element_type=jnp.float32
    ) * HD ** (-0.5)
    scores = jnp.where(allowed[None, None, :, :], scores, NEG)
    highest = jnp.max(scores, axis=-1, keepdims=True)
    exps = jnp.exp(scores - highest)
    totals = jnp.sum(exps, axis=-1)
    weights = exps.astype(jnp.bfloat16)
    mixed_rows = jnp.einsum(
        "kgqn,nkd->qkgd", weights, value_heads, preferred_element_type=jnp.float32
    )
    mixed_rows = mixed_rows / jnp.transpose(totals, (2, 0, 1))[..., None]
    log_total = highest[..., 0] + jnp.log(totals)
    log_rows = jnp.transpose(log_total, (2, 0, 1)).reshape(query_count, H)
    return (mixed_rows.reshape(query_count, model_width), log_rows)


def body_wide(
    queries,
    new_kv,
    cache_kv,
    cache_spans,
    recompute_rows,
    held_states,
    key_weight,
    norm_gain,
    routes,
    route_weights,
    expert_gate_up,
    expert_down,
):
    seq_index = lax.axis_index("seq")
    seq_count = lax.axis_size("seq")
    owner_count = lax.axis_size("req")
    req_rows, tok_rows, model_width = queries.shape
    cache_rows = cache_kv.shape[2]
    held_rows = held_states.shape[1]
    local_experts = expert_gate_up.shape[0]
    expert_total = owner_count * local_experts
    my_positions = lax.dynamic_slice_in_dim(recompute_rows, seq_index * held_rows, held_rows, 1)
    projected = jnp.dot(
        held_states.reshape(req_rows * held_rows, model_width),
        key_weight,
        preferred_element_type=jnp.float32,
    )
    rotated = rotate(projected.reshape(req_rows, held_rows, KVH, HD), my_positions)
    rotated = rotated.reshape(req_rows, held_rows, KVH * HD).astype(jnp.bfloat16)
    fresh_rows = lax.all_gather(rotated, "seq", axis=1, tiled=True)
    cache_positions = seq_index * cache_rows + jnp.arange(cache_rows)
    hit_table = recompute_rows[:, None, :] == cache_positions[None, :, None]
    placed = jnp.einsum(
        "rcm,rmk->rck",
        hit_table.astype(jnp.bfloat16),
        fresh_rows,
        preferred_element_type=jnp.float32,
    ).astype(jnp.bfloat16)
    cache_keys = jnp.where(jnp.any(hit_table, axis=2)[:, :, None], placed, cache_kv[0])
    span_start = cache_spans[:, 0:1]
    span_end = cache_spans[:, 1:2]
    all_queries = lax.all_gather(queries, "seq", axis=1, tiled=True)
    step_total = all_queries.shape[1]
    cache_allowed = (cache_positions[None, :] >= span_start) & (cache_positions[None, :] < span_end)
    key_positions = seq_index * tok_rows + jnp.arange(tok_rows)
    step_allowed = key_positions[None, :] <= jnp.arange(step_total)[:, None]
    allowed = jnp.concatenate(
        [
            jnp.broadcast_to(cache_allowed[:, None, :], (req_rows, step_total, cache_rows)),
            jnp.broadcast_to(step_allowed[None], (req_rows, step_total, tok_rows)),
        ],
        axis=2,
    )
    key_rows = jnp.concatenate([cache_keys, new_kv[0]], axis=1)
    value_rows = jnp.concatenate([cache_kv[1], new_kv[1]], axis=1)
    part_out, part_log = lax.map(partial_attend, (all_queries, key_rows, value_rows, allowed))
    piece_out, piece_log = (
        lax.all_to_all(part_out[None], "seq", split_axis=2, concat_axis=0, tiled=True),
        lax.all_to_all(part_log[None], "seq", split_axis=2, concat_axis=0, tiled=True),
    )
    best_log = jnp.max(piece_log, axis=0)
    factors = jnp.exp(piece_log - best_log[None])
    factor_sum = jnp.sum(factors, axis=0)
    spread_out = piece_out.reshape(seq_count, req_rows, tok_rows, H, HD)
    combined = jnp.sum(spread_out * factors[..., None], axis=0) / factor_sum[..., None]
    attended_f = combined.reshape(req_rows, tok_rows, model_width)
    attended = attended_f.astype(jnp.bfloat16)
    attended_f = attended.astype(jnp.float32)
    mean_square = jnp.mean(attended_f * attended_f, axis=-1, keepdims=True)
    normed = (attended_f * lax.rsqrt(mean_square + 1e-06) * norm_gain).astype(jnp.bfloat16)
    route_flat = routes.reshape(req_rows, tok_rows * TOP)
    expert_match = (route_flat[:, :, None] == jnp.arange(expert_total)[None, None, :]).astype(
        jnp.int32
    )
    order = jnp.arange(tok_rows * TOP)
    before = (order[None, :] < order[:, None]).astype(jnp.bfloat16)
    earlier = jnp.einsum(
        "ij,rje->rie",
        before,
        expert_match.astype(jnp.bfloat16),
        preferred_element_type=jnp.float32,
    ).astype(jnp.int32)
    slot_index = jnp.sum(earlier * expert_match, axis=2)
    target = route_flat * CAP + slot_index
    slot_match = target[:, :, None] == jnp.arange(expert_total * CAP)[None, None, :]
    dispatch = jnp.any(
        slot_match.reshape(req_rows, tok_rows, TOP, expert_total * CAP), axis=2
    ).astype(jnp.bfloat16)
    dispatch = dispatch.reshape(req_rows, tok_rows, owner_count, local_experts, CAP)
    outgoing = jnp.einsum(
        "rtnec,rtd->nrecd", dispatch, normed, preferred_element_type=jnp.float32
    ).astype(jnp.bfloat16)
    hidden = jnp.einsum(
        "srecd,edf->srecf",
        lax.all_to_all(outgoing, "req", split_axis=0, concat_axis=0, tiled=True),
        expert_gate_up,
        preferred_element_type=jnp.float32,
    )
    active = (jax.nn.silu(hidden[..., :FF]) * hidden[..., FF:]).astype(jnp.bfloat16)
    result = jnp.einsum(
        "srecf,efd->srecd", active, expert_down, preferred_element_type=jnp.float32
    ).astype(jnp.bfloat16)
    returned = lax.all_to_all(result, "req", split_axis=0, concat_axis=0, tiled=True)
    owner_of = route_flat // local_experts
    local_of = route_flat % local_experts
    flat_index = (
        (owner_of * req_rows + jnp.arange(req_rows)[:, None]) * local_experts + local_of
    ) * CAP + slot_index
    returned_rows = jnp.take(returned.reshape(-1, model_width), flat_index.reshape(-1), axis=0)
    returned_rows = returned_rows.reshape(req_rows, tok_rows, TOP, model_width)
    mixture = jnp.einsum(
        "rtk,rtkd->rtd",
        route_weights,
        returned_rows.astype(jnp.float32),
        precision=lax.Precision.HIGHEST,
    )
    return (attended_f + mixture).astype(jnp.bfloat16)


def layer_kernel(
    spans_ref,
    rec_ref,
    inverse_ref,
    gain_ref,
    routes_ref,
    rw_ref,
    q_hbm,
    new_hbm,
    cache_hbm,
    held_hbm,
    kw_hbm,
    gu_hbm,
    dn_hbm,
    out_ref,
    q_in,
    new_in,
    cache_in,
    held_in,
    kw_in,
    gu_v,
    dn_v,
    kvsend,
    stsend,
    qsend,
    fsend,
    osend,
    crecv,
    srecv,
    qrecv,
    frecv,
    orecv,
    placed,
    keep,
    att,
    trecv,
    wrecv,
    act,
    total,
    psend,
    precv,
    in_sem,
    load_sem,
    s_sem,
    r_sem,
    zs_sem,
    zr_sem,
    ts_sem,
    tr_sem,
):
    bf16 = jnp.bfloat16
    f32 = jnp.float32
    me = lax.axis_index("seq")
    S = lax.axis_size("seq")
    mz = lax.axis_index("req")
    N = lax.axis_size("req")
    groups = H // KVH
    tok = q_in.shape[1]
    crows = cache_in.shape[2]
    held = frecv.shape[0] // S
    width = q_in.shape[2]
    local_experts = gu_v.shape[0]
    stotal = S * tok
    lane = 2 * HD
    Q, NEW, FRESH, KV, OUT, Q1, NEW1 = 0, 1, 2, 3, 5, 7, 8
    near = mz + 1 - 2 * lax.rem(mz, 2)
    across = mz + 2 - 4 * (mz // 2)
    mirror = N - 1 - mz
    other = (mz, near, across, mirror)
    inner = (mz == 1) | (mz == 2)

    barrier = pltpu.get_barrier_semaphore()
    for k in range(1, S):
        pl.semaphore_signal(barrier, inc=1, device_id={"seq": lax.rem(me + k, S)})
    for k in range(1, N):
        pl.semaphore_signal(barrier, inc=1, device_id={"req": lax.rem(mz + k, N)})

    inputs = [
        pltpu.make_async_copy(src, dst, in_sem.at[i])
        for i, (src, dst) in enumerate(
            (
                (q_hbm, q_in),
                (new_hbm, new_in),
                (held_hbm, held_in),
                (kw_hbm, kw_in),
                (cache_hbm.at[:, 0], cache_in.at[0]),
                (cache_hbm.at[:, 1], cache_in.at[1]),
            )
        )
    ]
    for copy in inputs:
        copy.start()

    def lanes(rows):
        return lax.broadcasted_iota(jnp.int32, (rows, lane), 1)

    def swap(x):
        return pltpu.roll(x, HD, 1)

    def merge(low, high):
        return jnp.where(lanes(low.shape[0]) < HD, low, high)

    def join(low, low_roll, high, high_roll, scale=None):
        a, b = low.astype(f32), high.astype(f32)
        a = swap(a) if low_roll else a
        b = swap(b) if high_roll else b
        c = merge(a, b)
        return (c if scale is None else c * scale).astype(bf16)

    def pair_cols(h):
        return slice((h // 2) * lane, (h // 2 + 1) * lane), h % 2 == 1

    def row_at(i, n):
        return pl.ds(pl.multiple_of(i * n, n), n)

    def exchange(kind, k, slot):
        peer = lax.rem(me + k, S)
        src, dst = (
            (qsend.at[0, peer], qrecv.at[0, slot]),
            (stsend.at[0, peer], srecv.at[0, row_at(slot, tok), :]),
            (fsend.at[peer], frecv.at[row_at(slot, held), :]),
            (kvsend.at[0, peer], crecv.at[0, slot]),
            (kvsend.at[1, peer], crecv.at[1, slot]),
            (osend.at[0, peer], orecv.at[0, slot]),
            (osend.at[1, peer], orecv.at[1, slot]),
            (qsend.at[1, peer], qrecv.at[1, slot]),
            (stsend.at[1, peer], srecv.at[1, row_at(slot, tok), :]),
        )[kind]
        return pltpu.make_async_remote_copy(
            src_ref=src,
            dst_ref=dst,
            send_sem=s_sem.at[kind, k],
            recv_sem=r_sem.at[kind, k],
            device_id={"seq": peer},
        )

    def send(kind, steps=None):
        for k in range(1, S) if steps is None else steps:
            exchange(kind, k, me).start()

    def arrive_from(kind, k):
        exchange(kind, k, lax.rem(me + S - k, S)).wait_recv()

    def arrive(kind):
        for k in range(1, S):
            arrive_from(kind, k)

    inputs[0].wait()
    inputs[1].wait()
    half_tok = tok // 2

    def pack_step(r):
        for h in range(KVH):
            cols, odd = pair_cols(h)
            tiles = [(q_in[r, :, pair_cols(c)[0]], pair_cols(c)[1]) for c in range(3 * h, 3 * h + 3)]
            (one, one_odd), (two, two_odd), (last, last_odd) = tiles
            qsend[r, h, :tok] = join(one, one_odd, two, not two_odd, HD**-0.5)
            qsend[r, h, tok:] = join(
                last[:half_tok], last_odd, last[half_tok:], not last_odd, HD**-0.5
            )
            keys, values = new_in[0, r, :, cols], new_in[1, r, :, cols]
            low, high = (keys, values) if r == 0 else (values, keys)
            stsend[r, h] = join(low, odd, high, not odd)

    pack_step(0)

    pl.semaphore_wait(barrier, S - 1 + N - 1)
    send(Q)
    send(NEW)

    def pack_cache(r):
        inputs[4 + r].wait()
        for h in range(KVH):
            cols, odd = pair_cols(h)
            keys, values = cache_in[r, 0, :, cols], cache_in[r, 1, :, cols]
            low, high = (keys, values) if r == 0 else (values, keys)
            kvsend[r, h] = join(low, odd, high, not odd)


    inputs[2].wait()
    inputs[3].wait()
    fresh = jnp.dot(held_in[...], kw_in[...], preferred_element_type=f32)
    low_part = lax.broadcasted_iota(jnp.int32, fresh.shape, 1) % HD < HD // 2
    partner = jnp.where(
        low_part,
        pltpu.roll(fresh, fresh.shape[1] - HD // 2, 1),
        pltpu.roll(fresh, HD // 2, 1),
    )
    row_lane = lax.broadcasted_iota(jnp.int32, (held, S * held), 1)
    row_here = lax.broadcasted_iota(jnp.int32, (held, S * held), 0) + me * held
    positions = jnp.concatenate(
        [
            jnp.sum(
                jnp.where(row_lane == row_here, rec_ref[r : r + 1, :].astype(f32), 0.0),
                axis=1,
                keepdims=True,
            )
            for r in range(2)
        ],
        axis=0,
    )
    angles = positions * inverse_ref[...]
    cos_table, sin_table = jnp.cos(angles), jnp.sin(angles)
    sin_table = jnp.where(lanes(2 * held) % HD < HD // 2, -sin_table, sin_table)
    fresh = fresh * jnp.tile(cos_table, (1, KVH // 2)) + partner * jnp.tile(
        sin_table, (1, KVH // 2)
    )
    for h in range(KVH):
        cols, odd = pair_cols(h)
        fsend[h] = join(fresh[:held, cols], odd, fresh[held:, cols], not odd)
    send(FRESH)
    pack_cache(0)
    send(KV)

    loads = []
    for e in range(local_experts):
        loads.append(pltpu.make_async_copy(gu_hbm.at[e], gu_v.at[e], load_sem.at[0, e]))
    for e in range(local_experts):
        loads.append(pltpu.make_async_copy(dn_hbm.at[e], dn_v.at[e], load_sem.at[1, e]))
    for load in loads:
        load.start()

    pack_step(1)
    pack_cache(1)

    expert_row = lax.broadcasted_iota(jnp.int32, (128, tok), 0)
    for r in range(2):
        dense = jnp.zeros((128, tok), f32)
        for k in range(TOP):
            hit = routes_ref[r, k : k + 1, :] == expert_row
            dense = dense + jnp.where(hit, rw_ref[r, k : k + 1, :], 0.0)
        wrecv[mz, r * tok : (r + 1) * tok, :] = dense.T

    def share_copy(k, slot):
        return pltpu.make_async_remote_copy(
            src_ref=wrecv.at[mz],
            dst_ref=wrecv.at[slot],
            send_sem=zs_sem.at[0, k],
            recv_sem=zr_sem.at[0, k],
            device_id={"req": lax.rem(mz + k, N)},
        )

    def back_copy(r, half, block, to, slot):
        return pltpu.make_async_remote_copy(
            src_ref=psend.at[r, half, other[block]],
            dst_ref=precv.at[r, half, slot],
            send_sem=zs_sem.at[1 + 2 * r + half, block],
            recv_sem=zr_sem.at[1 + 2 * r + half, slot],
            device_id={"req": other[to]},
        )

    def token_copy(r, origin, to, way):
        return pltpu.make_async_remote_copy(
            src_ref=trecv.at[r, origin],
            dst_ref=trecv.at[r, origin],
            send_sem=ts_sem.at[r, way],
            recv_sem=tr_sem.at[r, origin],
            device_id={"req": other[to]},
        )

    def send_tokens(r):
        token_copy(r, mz, 2, 2).start()

        @pl.when(inner)
        def _():
            token_copy(r, mz, 3, 3).start()

        token_copy(r, mz, 1, 1).start()

    def relay_tokens(r):
        token_copy(r, across, 1, 0).wait_recv()

        @pl.when(inner)
        def _():
            token_copy(r, across, 1, 0).start()

    def rest_of_tokens(r):
        token_copy(r, near, 1, 0).wait_recv()
        token_copy(r, mirror, 1, 0).wait_recv()

    def send_back(r, half):
        @pl.when(jnp.logical_not(inner))
        def _():
            back_copy(r, half, 3, 1, 0).start()
            back_copy(r, half, 2, 2, 2).start()

    def send_back_near(r):
        for half in range(2):

            @pl.when(inner)
            def _():
                back_copy(r, half, 1, 1, 1).start()
                back_copy(r, half, 3, 3, 3).start()

            @pl.when(jnp.logical_not(inner))
            def _():
                back_copy(r, half, 1, 1, 1).start()

    def relay_back(r, half):
        @pl.when(inner)
        def _():
            back_copy(r, half, 3, 1, 0).wait_recv()
            both = psend[r, half, across].astype(f32) + precv[r, half, 0].astype(f32)
            psend[r, half, across] = both.astype(bf16)
            back_copy(r, half, 2, 2, 2).start()

    for k in range(1, N):
        share_copy(k, mz).start()

    for r in range(2):
        qrecv[r, me] = qsend[r, me]
        srecv[r, row_at(me, tok), :] = stsend[r, me]
    frecv[row_at(me, held), :] = fsend[me]
    arrive(Q)
    arrive(NEW)
    arrive(FRESH)
    ones = jnp.ones((S * held, lane), bf16)
    spread = jnp.concatenate([frecv[...], ones], axis=1)

    def place_fresh(r):
        wanted = rec_ref[r : r + 1, :]

        def place(i, carry):
            where_to = lax.broadcasted_iota(jnp.int32, (crows, S * held), 0) + i * crows
            hit = jnp.where(where_to == wanted, 1.0, 0.0).astype(bf16)
            both = jnp.dot(hit, spread, preferred_element_type=f32)
            placed[r, i] = both[:, :lane].astype(bf16)
            keep[r, i] = (1.0 - both[:, lane:]).astype(bf16)
            return carry

        lax.fori_loop(0, S, place, 0)

    def pass_on(sent, steps):
        for k in sent:
            exchange(KV, k, me).wait_send()
        send(KV + 1, steps)

    place_fresh(0)
    for k in range(1, 5):
        exchange(KV, k, me).wait_send()
    send(Q1)
    send(NEW1)
    send(KV + 1, (1, 2))

    contract = (((1,), (1,)), ((), ()))

    def key_lanes(r, rows):
        return lanes(rows) < HD if r == 0 else lanes(rows) >= HD

    def chunk(r, state, query, keys, raw, bias=None, mask=None):
        scores = lax.dot_general(query, keys, contract, preferred_element_type=f32)
        if bias is not None:
            scores = scores + bias
        if mask is not None:
            scores = jnp.where(mask, scores, NEG)
        values = jnp.where(key_lanes(r, raw.shape[0]), jnp.ones_like(raw), raw)
        highest = jnp.max(scores, axis=-1, keepdims=True)
        if state is None:
            exps = jnp.exp(scores - highest).astype(bf16)
            return highest, jnp.dot(exps, values, preferred_element_type=f32)
        before, mixed = state
        highest = jnp.maximum(before, highest)
        exps = jnp.exp(scores - highest).astype(bf16)
        mixed = mixed * jnp.exp(before - highest)
        return highest, mixed + jnp.dot(exps, values, preferred_element_type=f32)

    def query_of(r):
        two = qrecv[r, :, :tok, :].reshape(stotal, lane).astype(f32)
        last = qrecv[r, :, tok:, :].reshape(S * half_tok, lane).astype(f32)
        first = two if r == 0 else swap(two)
        second = swap(two) if r == 0 else two
        early = last if r == 0 else swap(last)
        later = swap(last) if r == 0 else last
        third = jnp.concatenate(
            [early.reshape(S, half_tok, lane), later.reshape(S, half_tok, lane)], axis=1
        ).reshape(stotal, lane)
        query = jnp.concatenate([first, second, third], axis=0)
        return jnp.where(key_lanes(r, groups * stotal), query, 0.0).astype(bf16)

    def attend_new(r, query):
        rows = lax.broadcasted_iota(jnp.int32, (groups * stotal, stotal), 0) % stotal
        causal = lax.broadcasted_iota(jnp.int32, (groups * stotal, stotal), 1) <= rows
        return chunk(r, None, query, srecv[r], srecv[r], mask=causal)

    def attend_cache(r, state, query, k):
        source = lax.rem(me + S - k, S)
        raw = kvsend[r, source] if k == 0 else crecv[r, source]
        keys = placed[r, source] + keep[r, source] * raw
        position = lax.broadcasted_iota(jnp.int32, (1, crows), 1) + source * crows
        open_row = (position >= spans_ref[r, 0]) & (position < spans_ref[r, 1])
        return chunk(r, state, query, keys, raw, bias=jnp.where(open_row, 0.0, NEG))

    def finish(r, state):
        mixed = state[1]
        mixed = mixed / swap(mixed)
        turned = swap(mixed)
        low, high = (turned, mixed) if r == 0 else (mixed, turned)
        head = [slice(g * stotal, (g + 1) * stotal) for g in range(groups)]
        two = merge(low[head[0]], high[head[1]]).astype(bf16)
        osend[r, :, :tok, :] = two.reshape(S, tok, lane)
        half = tok // 2
        one_low = low[head[2]].reshape(S, tok, lane)[:, :half].reshape(S * half, lane)
        one_high = high[head[2]].reshape(S, tok, lane)[:, half:].reshape(S * half, lane)
        osend[r, :, tok:, :] = merge(one_low, one_high).astype(bf16).reshape(S, half, lane)
        send(OUT + r)
        orecv[r, me] = osend[r, me]

    def gather_heads(r):
        arrive(OUT + r)
        for p in range(S // 2):
            even, odd = orecv[r, 2 * p].astype(f32), orecv[r, 2 * p + 1].astype(f32)
            even_solo, odd_solo = even[tok:], odd[tok:]
            odd_two = swap(odd[:tok])
            tile_b = merge(jnp.concatenate([even_solo, swap(even_solo)], axis=0), odd_two)
            tile_c = merge(odd_two, jnp.concatenate([swap(odd_solo), odd_solo], axis=0))
            att[r, :, p * 3 * lane : (p + 1) * 3 * lane] = jnp.concatenate(
                [even[:tok], tile_b, tile_c], axis=1
            )
        attended = att[r]
        mean_square = jnp.mean(attended * attended, axis=-1, keepdims=True)
        gain = gain_ref[...].reshape(1, width)
        trecv[r, mz] = (attended * lax.rsqrt(mean_square + 1e-06) * gain).astype(bf16)
        send_tokens(r)

    query = query_of(0)
    state = attend_new(0, query)
    state = attend_cache(0, state, query, 0)
    pass_on(range(5, S), (3, 4))
    arrive(KV)
    for k in range(1, S):
        state = attend_cache(0, state, query, k)
    finish(0, state)
    send(KV + 1, range(5, S))

    place_fresh(1)
    arrive(Q1)
    arrive(NEW1)
    query = query_of(1)
    state = attend_new(1, query)
    state = attend_cache(1, state, query, 0)
    for part in ((1, 2), (3, 4), (5, 6, 7)):
        for k in part:
            arrive_from(KV + 1, k)
        for k in part:
            state = attend_cache(1, state, query, k)
        if part[0] == 1:
            gather_heads(0)
    finish(1, state)
    relay_tokens(0)
    gather_heads(1)
    rest_of_tokens(0)
    for k in range(1, N):
        share_copy(k, lax.rem(mz + N - k, N)).wait_recv()

    rows_total = N * tok
    part_width = width // 2

    def experts(r):
        tokens = trecv[r].reshape(rows_total, width)
        weights = wrecv[:, r * tok : (r + 1) * tok, :].reshape(rows_total, 128)
        column = lax.broadcasted_iota(jnp.int32, weights.shape, 1)
        for e in range(local_experts):
            if r == 0:
                loads[e].wait()
            hidden = jnp.dot(tokens, gu_v[e], preferred_element_type=f32)
            gate, up = hidden[:, :FF], hidden[:, FF:]
            share = jnp.sum(
                jnp.where(column == mz * local_experts + e, weights, 0.0), axis=1, keepdims=True
            )
            act[:, e * FF : (e + 1) * FF] = (gate / (1.0 + jnp.exp(-gate)) * up * share).astype(
                bf16
            )
        if r == 0:
            for load in loads[local_experts:]:
                load.wait()
        down = dn_v[...].reshape(local_experts * FF, width)
        for half in range(2):
            summed = jnp.dot(
                act[...],
                down[:, half * part_width : (half + 1) * part_width],
                preferred_element_type=f32,
            )
            psend[r, half] = summed.astype(bf16).reshape(N, tok, part_width)
            send_back(r, half)
        send_back_near(r)

    experts(0)
    relay_tokens(1)
    for half in range(2):
        relay_back(0, half)
    rest_of_tokens(1)
    experts(1)
    for half in range(2):
        relay_back(1, half)
    for r in range(2):
        for half in range(2):
            cols = slice(half * part_width, (half + 1) * part_width)
            back_copy(r, half, 1, 1, 1).wait_recv()
            back_copy(r, half, 2, 2, 2).wait_recv()
            mixture = att[r, :, cols] + psend[r, half, mz].astype(f32)
            mixture = mixture + precv[r, half, 1].astype(f32) + precv[r, half, 2].astype(f32)
            total[r, :, cols] = mixture

            @pl.when(inner)
            def _():
                back_copy(r, half, 3, 3, 3).wait_recv()
                total[r, :, cols] += precv[r, half, 3].astype(f32)

            out_ref[r * tok : (r + 1) * tok, cols] = total[r, :, cols].astype(bf16)
    for kind in (Q, NEW, FRESH, KV + 1, OUT, OUT + 1, Q1, NEW1):
        for k in range(1, S):
            exchange(kind, k, me).wait_send()
    for k in range(1, N):
        share_copy(k, mz).wait_send()
    for r in range(2):
        for half in range(2):
            for block in (1, 2, 3):
                back_copy(r, half, block, 1, 1).wait_send()
        for way in (1, 2):
            token_copy(r, mz, 1, way).wait_send()

        @pl.when(inner)
        def _():
            token_copy(r, mz, 3, 3).wait_send()
            token_copy(r, across, 1, 0).wait_send()


def head_parallel_body(
    queries,
    new_kv,
    cache_kv,
    cache_spans,
    recompute_rows,
    held_states,
    key_weight,
    norm_gain,
    routes,
    route_weights,
    expert_gate_up,
    expert_down,
):
    S = lax.axis_size("seq")
    N = lax.axis_size("req")
    req_rows, tok, width = queries.shape
    crows = cache_kv.shape[2]
    held = held_states.shape[1]
    local_experts = expert_gate_up.shape[0]
    groups = H // KVH
    bf16, f32 = jnp.bfloat16, jnp.float32
    half = HD // 2
    inverse = THETA ** (-((np.arange(2 * HD) % half) * (2.0 / HD)))
    inverse = jnp.asarray(inverse.astype(np.float32).reshape(1, 2 * HD))
    vmem = pl.BlockSpec(memory_space=pltpu.VMEM)
    smem = pl.BlockSpec(memory_space=pltpu.SMEM)
    hbm = pl.BlockSpec(memory_space=pl.ANY)
    lane = 2 * HD
    rows = req_rows * tok
    out = pl.pallas_call(
        layer_kernel,
        out_shape=pltpu.VMEM((rows, width), bf16),
        in_specs=[smem] + [vmem] * 5 + [hbm] * 7,
        out_specs=vmem,
        scratch_shapes=[
            pltpu.VMEM((req_rows, tok, width), bf16),
            pltpu.VMEM((2, req_rows, tok, KVH * HD), bf16),
            pltpu.VMEM((req_rows, 2, crows, KVH * HD), bf16),
            pltpu.VMEM((req_rows * held, width), bf16),
            pltpu.VMEM(key_weight.shape, bf16),
            pltpu.VMEM(expert_gate_up.shape, bf16),
            pltpu.VMEM(expert_down.shape, bf16),
            pltpu.VMEM((2, S, crows, lane), bf16),
            pltpu.VMEM((2, S, tok, lane), bf16),
            pltpu.VMEM((2, S, tok * 3 // 2, lane), bf16),
            pltpu.VMEM((S, held, lane), bf16),
            pltpu.VMEM((2, S, tok * 3 // 2, lane), bf16),
            pltpu.VMEM((2, S, crows, lane), bf16),
            pltpu.VMEM((2, S * tok, lane), bf16),
            pltpu.VMEM((2, S, tok * 3 // 2, lane), bf16),
            pltpu.VMEM((S * held, lane), bf16),
            pltpu.VMEM((2, S, tok * 3 // 2, lane), bf16),
            pltpu.VMEM((2, S, crows, lane), bf16),
            pltpu.VMEM((2, S, crows, lane), bf16),
            pltpu.VMEM((2, tok, width), f32),
            pltpu.VMEM((2, N, tok, width), bf16),
            pltpu.VMEM((N, rows, 128), f32),
            pltpu.VMEM((N * tok, local_experts * FF), bf16),
            pltpu.VMEM((2, tok, width), f32),
            pltpu.VMEM((2, 2, N, tok, width // 2), bf16),
            pltpu.VMEM((2, 2, N, tok, width // 2), bf16),
            pltpu.SemaphoreType.DMA((6,)),
            pltpu.SemaphoreType.DMA((2, local_experts)),
            pltpu.SemaphoreType.DMA((9, S)),
            pltpu.SemaphoreType.DMA((9, S)),
            pltpu.SemaphoreType.DMA((5, N)),
            pltpu.SemaphoreType.DMA((5, N)),
            pltpu.SemaphoreType.DMA((2, N)),
            pltpu.SemaphoreType.DMA((2, N)),
        ],
        compiler_params=pltpu.CompilerParams(
            collective_id=0, has_side_effects=True, vmem_limit_bytes=60 << 20
        ),
        name="layer",
    )(
        cache_spans,
        recompute_rows,
        inverse,
        norm_gain,
        jnp.transpose(routes, (0, 2, 1)),
        jnp.transpose(route_weights, (0, 2, 1)),
        queries,
        new_kv,
        cache_kv,
        held_states.reshape(req_rows * held, width),
        key_weight,
        expert_gate_up,
        expert_down,
    )
    return out.reshape(req_rows, tok, width)


def solution(mesh):
    by_heads = mesh.shape["seq"] == KVH and mesh.shape["req"] == 4
    body = head_parallel_body if by_heads else body_wide
    in_specs = (
        P("req", "seq", None),
        P(None, "req", "seq", None),
        P(None, "req", "seq", None),
        P("req", None),
        P("req", None),
        P("req", "seq", None),
        P(),
        P(),
        P("req", "seq", None),
        P("req", "seq", None),
        P("req", None, None),
        P("req", None, None),
    )
    out_specs = P("req", "seq", None)
    return jax.shard_map(body, mesh=mesh, in_specs=in_specs, out_specs=out_specs, check_vma=False)
```

```python
import jax
import jax.numpy as jnp
import numpy as np
from jax import lax
from jax.experimental import pallas as pl
from jax.experimental.pallas import tpu as pltpu
from jax.sharding import PartitionSpec as P

H = 24
KVH = 8
HD = 64
FF = 512
TOP = 8
CAP = 16


NEG = -1e30
THETA = 10000.0


def rotate(key_heads, positions):
    half_dim = key_heads.shape[-1] // 2
    exponent = jnp.arange(half_dim).astype(jnp.float32) * (2.0 / key_heads.shape[-1])
    inverse = THETA ** (-exponent)
    angles = positions.astype(jnp.float32)[..., None] * inverse
    cosine = jnp.cos(angles)[..., None, :]
    sine_part = jnp.sin(angles)[..., None, :]
    lower_half = key_heads[..., :half_dim]
    upper_half = key_heads[..., half_dim:]
    return jnp.concatenate(
        [
            lower_half * cosine - upper_half * sine_part,
            upper_half * cosine + lower_half * sine_part,
        ],
        axis=-1,
    )


def partial_attend(packed):
    query_rows, key_rows, value_rows, allowed = packed
    query_count, model_width = query_rows.shape
    key_count = key_rows.shape[0]
    groups = H // KVH
    query_heads = query_rows.reshape(query_count, KVH, groups, HD)
    key_heads = key_rows.reshape(key_count, KVH, HD)
    value_heads = value_rows.reshape(key_count, KVH, HD)
    scores = jnp.einsum(
        "qkgd,nkd->kgqn", query_heads, key_heads, preferred_element_type=jnp.float32
    ) * HD ** (-0.5)
    scores = jnp.where(allowed[None, None, :, :], scores, NEG)
    highest = jnp.max(scores, axis=-1, keepdims=True)
    exps = jnp.exp(scores - highest)
    totals = jnp.sum(exps, axis=-1)
    weights = exps.astype(jnp.bfloat16)
    mixed_rows = jnp.einsum(
        "kgqn,nkd->qkgd", weights, value_heads, preferred_element_type=jnp.float32
    )
    mixed_rows = mixed_rows / jnp.transpose(totals, (2, 0, 1))[..., None]
    log_total = highest[..., 0] + jnp.log(totals)
    log_rows = jnp.transpose(log_total, (2, 0, 1)).reshape(query_count, H)
    return (mixed_rows.reshape(query_count, model_width), log_rows)


def body_wide(
    queries,
    new_kv,
    cache_kv,
    cache_spans,
    recompute_rows,
    held_states,
    key_weight,
    norm_gain,
    routes,
    route_weights,
    expert_gate_up,
    expert_down,
):
    seq_index = lax.axis_index("seq")
    seq_count = lax.axis_size("seq")
    owner_count = lax.axis_size("req")
    req_rows, tok_rows, model_width = queries.shape
    cache_rows = cache_kv.shape[2]
    held_rows = held_states.shape[1]
    local_experts = expert_gate_up.shape[0]
    expert_total = owner_count * local_experts
    my_positions = lax.dynamic_slice_in_dim(recompute_rows, seq_index * held_rows, held_rows, 1)
    projected = jnp.dot(
        held_states.reshape(req_rows * held_rows, model_width),
        key_weight,
        preferred_element_type=jnp.float32,
    )
    rotated = rotate(projected.reshape(req_rows, held_rows, KVH, HD), my_positions)
    rotated = rotated.reshape(req_rows, held_rows, KVH * HD).astype(jnp.bfloat16)
    fresh_rows = lax.all_gather(rotated, "seq", axis=1, tiled=True)
    cache_positions = seq_index * cache_rows + jnp.arange(cache_rows)
    hit_table = recompute_rows[:, None, :] == cache_positions[None, :, None]
    placed = jnp.einsum(
        "rcm,rmk->rck",
        hit_table.astype(jnp.bfloat16),
        fresh_rows,
        preferred_element_type=jnp.float32,
    ).astype(jnp.bfloat16)
    cache_keys = jnp.where(jnp.any(hit_table, axis=2)[:, :, None], placed, cache_kv[0])
    span_start = cache_spans[:, 0:1]
    span_end = cache_spans[:, 1:2]
    all_queries = lax.all_gather(queries, "seq", axis=1, tiled=True)
    step_total = all_queries.shape[1]
    cache_allowed = (cache_positions[None, :] >= span_start) & (cache_positions[None, :] < span_end)
    key_positions = seq_index * tok_rows + jnp.arange(tok_rows)
    step_allowed = key_positions[None, :] <= jnp.arange(step_total)[:, None]
    allowed = jnp.concatenate(
        [
            jnp.broadcast_to(cache_allowed[:, None, :], (req_rows, step_total, cache_rows)),
            jnp.broadcast_to(step_allowed[None], (req_rows, step_total, tok_rows)),
        ],
        axis=2,
    )
    key_rows = jnp.concatenate([cache_keys, new_kv[0]], axis=1)
    value_rows = jnp.concatenate([cache_kv[1], new_kv[1]], axis=1)
    part_out, part_log = lax.map(partial_attend, (all_queries, key_rows, value_rows, allowed))
    piece_out, piece_log = (
        lax.all_to_all(part_out[None], "seq", split_axis=2, concat_axis=0, tiled=True),
        lax.all_to_all(part_log[None], "seq", split_axis=2, concat_axis=0, tiled=True),
    )
    best_log = jnp.max(piece_log, axis=0)
    factors = jnp.exp(piece_log - best_log[None])
    factor_sum = jnp.sum(factors, axis=0)
    spread_out = piece_out.reshape(seq_count, req_rows, tok_rows, H, HD)
    combined = jnp.sum(spread_out * factors[..., None], axis=0) / factor_sum[..., None]
    attended_f = combined.reshape(req_rows, tok_rows, model_width)
    attended = attended_f.astype(jnp.bfloat16)
    attended_f = attended.astype(jnp.float32)
    mean_square = jnp.mean(attended_f * attended_f, axis=-1, keepdims=True)
    normed = (attended_f * lax.rsqrt(mean_square + 1e-06) * norm_gain).astype(jnp.bfloat16)
    route_flat = routes.reshape(req_rows, tok_rows * TOP)
    expert_match = (route_flat[:, :, None] == jnp.arange(expert_total)[None, None, :]).astype(
        jnp.int32
    )
    order = jnp.arange(tok_rows * TOP)
    before = (order[None, :] < order[:, None]).astype(jnp.bfloat16)
    earlier = jnp.einsum(
        "ij,rje->rie",
        before,
        expert_match.astype(jnp.bfloat16),
        preferred_element_type=jnp.float32,
    ).astype(jnp.int32)
    slot_index = jnp.sum(earlier * expert_match, axis=2)
    target = route_flat * CAP + slot_index
    slot_match = target[:, :, None] == jnp.arange(expert_total * CAP)[None, None, :]
    dispatch = jnp.any(
        slot_match.reshape(req_rows, tok_rows, TOP, expert_total * CAP), axis=2
    ).astype(jnp.bfloat16)
    dispatch = dispatch.reshape(req_rows, tok_rows, owner_count, local_experts, CAP)
    outgoing = jnp.einsum(
        "rtnec,rtd->nrecd", dispatch, normed, preferred_element_type=jnp.float32
    ).astype(jnp.bfloat16)
    hidden = jnp.einsum(
        "srecd,edf->srecf",
        lax.all_to_all(outgoing, "req", split_axis=0, concat_axis=0, tiled=True),
        expert_gate_up,
        preferred_element_type=jnp.float32,
    )
    active = (jax.nn.silu(hidden[..., :FF]) * hidden[..., FF:]).astype(jnp.bfloat16)
    result = jnp.einsum(
        "srecf,efd->srecd", active, expert_down, preferred_element_type=jnp.float32
    ).astype(jnp.bfloat16)
    returned = lax.all_to_all(result, "req", split_axis=0, concat_axis=0, tiled=True)
    owner_of = route_flat // local_experts
    local_of = route_flat % local_experts
    flat_index = (
        (owner_of * req_rows + jnp.arange(req_rows)[:, None]) * local_experts + local_of
    ) * CAP + slot_index
    returned_rows = jnp.take(returned.reshape(-1, model_width), flat_index.reshape(-1), axis=0)
    returned_rows = returned_rows.reshape(req_rows, tok_rows, TOP, model_width)
    mixture = jnp.einsum(
        "rtk,rtkd->rtd",
        route_weights,
        returned_rows.astype(jnp.float32),
        precision=lax.Precision.HIGHEST,
    )
    return (attended_f + mixture).astype(jnp.bfloat16)


def layer_kernel(
    spans_ref,
    rec_ref,
    inverse_ref,
    gain_ref,
    routes_ref,
    rw_ref,
    q_hbm,
    new_hbm,
    cache_hbm,
    held_hbm,
    kw_hbm,
    gu_hbm,
    dn_hbm,
    out_ref,
    q_in,
    new_in,
    cache_in,
    held_in,
    kw_in,
    gu_v,
    dn_v,
    kvsend,
    stsend,
    qsend,
    fsend,
    osend,
    crecv,
    srecv,
    qrecv,
    frecv,
    orecv,
    placed,
    keep,
    att,
    trecv,
    wrecv,
    act,
    total,
    psend,
    precv,
    in_sem,
    load_sem,
    s_sem,
    r_sem,
    zs_sem,
    zr_sem,
    ts_sem,
    tr_sem,
):
    bf16 = jnp.bfloat16
    f32 = jnp.float32
    me = lax.axis_index("seq")
    S = lax.axis_size("seq")
    mz = lax.axis_index("req")
    N = lax.axis_size("req")
    groups = H // KVH
    tok = q_in.shape[1]
    crows = cache_in.shape[2]
    held = frecv.shape[0] // S
    width = q_in.shape[2]
    local_experts = gu_v.shape[0]
    stotal = S * tok
    lane = 2 * HD
    Q, NEW, FRESH, KV, OUT, Q1, NEW1 = 0, 1, 2, 3, 5, 7, 8
    near = mz + 1 - 2 * lax.rem(mz, 2)
    across = mz + 2 - 4 * (mz // 2)
    mirror = N - 1 - mz
    other = (mz, near, across, mirror)
    inner = (mz == 1) | (mz == 2)

    barrier = pltpu.get_barrier_semaphore()
    for k in range(1, S):
        pl.semaphore_signal(barrier, inc=1, device_id={"seq": lax.rem(me + k, S)})
    for k in range(1, N):
        pl.semaphore_signal(barrier, inc=1, device_id={"req": lax.rem(mz + k, N)})

    inputs = [
        pltpu.make_async_copy(src, dst, in_sem.at[i])
        for i, (src, dst) in enumerate(
            (
                (q_hbm, q_in),
                (new_hbm, new_in),
                (held_hbm, held_in),
                (kw_hbm, kw_in),
                (cache_hbm.at[:, 0], cache_in.at[0]),
                (cache_hbm.at[:, 1], cache_in.at[1]),
            )
        )
    ]
    for copy in inputs:
        copy.start()

    def lanes(rows):
        return lax.broadcasted_iota(jnp.int32, (rows, lane), 1)

    def swap(x):
        return pltpu.roll(x, HD, 1)

    def merge(low, high):
        return jnp.where(lanes(low.shape[0]) < HD, low, high)

    def join(low, low_roll, high, high_roll, scale=None):
        a, b = low.astype(f32), high.astype(f32)
        a = swap(a) if low_roll else a
        b = swap(b) if high_roll else b
        c = merge(a, b)
        return (c if scale is None else c * scale).astype(bf16)

    def pair_cols(h):
        return slice((h // 2) * lane, (h // 2 + 1) * lane), h % 2 == 1

    def row_at(i, n):
        return pl.ds(pl.multiple_of(i * n, n), n)

    def exchange(kind, k, slot):
        peer = lax.rem(me + k, S)
        src, dst = (
            (qsend.at[0, peer], qrecv.at[0, slot]),
            (stsend.at[0, peer], srecv.at[0, row_at(slot, tok), :]),
            (fsend.at[peer], frecv.at[row_at(slot, held), :]),
            (kvsend.at[0, peer], crecv.at[0, slot]),
            (kvsend.at[1, peer], crecv.at[1, slot]),
            (osend.at[0, peer], orecv.at[0, slot]),
            (osend.at[1, peer], orecv.at[1, slot]),
            (qsend.at[1, peer], qrecv.at[1, slot]),
            (stsend.at[1, peer], srecv.at[1, row_at(slot, tok), :]),
        )[kind]
        return pltpu.make_async_remote_copy(
            src_ref=src,
            dst_ref=dst,
            send_sem=s_sem.at[kind, k],
            recv_sem=r_sem.at[kind, k],
            device_id={"seq": peer},
        )

    def send(kind, steps=None):
        for k in range(1, S) if steps is None else steps:
            exchange(kind, k, me).start()

    def arrive_from(kind, k):
        exchange(kind, k, lax.rem(me + S - k, S)).wait_recv()

    def arrive(kind):
        for k in range(1, S):
            arrive_from(kind, k)

    inputs[0].wait()
    inputs[1].wait()
    half_tok = tok // 2

    def pack_step(r):
        for h in range(KVH):
            cols, odd = pair_cols(h)
            tiles = [(q_in[r, :, pair_cols(c)[0]], pair_cols(c)[1]) for c in range(3 * h, 3 * h + 3)]
            (one, one_odd), (two, two_odd), (last, last_odd) = tiles
            qsend[r, h, :tok] = join(one, one_odd, two, not two_odd, HD**-0.5)
            qsend[r, h, tok:] = join(
                last[:half_tok], last_odd, last[half_tok:], not last_odd, HD**-0.5
            )
            keys, values = new_in[0, r, :, cols], new_in[1, r, :, cols]
            low, high = (keys, values) if r == 0 else (values, keys)
            stsend[r, h] = join(low, odd, high, not odd)

    pack_step(0)

    def pack_cache(r):
        inputs[4 + r].wait()
        for h in range(KVH):
            cols, odd = pair_cols(h)
            keys, values = cache_in[r, 0, :, cols], cache_in[r, 1, :, cols]
            low, high = (keys, values) if r == 0 else (values, keys)
            kvsend[r, h] = join(low, odd, high, not odd)


    pack_cache(0)
    pl.semaphore_wait(barrier, S - 1 + N - 1)
    send(Q)
    send(NEW)

    inputs[2].wait()
    inputs[3].wait()
    fresh = jnp.dot(held_in[...], kw_in[...], preferred_element_type=f32)
    low_part = lax.broadcasted_iota(jnp.int32, fresh.shape, 1) % HD < HD // 2
    partner = jnp.where(
        low_part,
        pltpu.roll(fresh, fresh.shape[1] - HD // 2, 1),
        pltpu.roll(fresh, HD // 2, 1),
    )
    row_lane = lax.broadcasted_iota(jnp.int32, (held, S * held), 1)
    row_here = lax.broadcasted_iota(jnp.int32, (held, S * held), 0) + me * held
    positions = jnp.concatenate(
        [
            jnp.sum(
                jnp.where(row_lane == row_here, rec_ref[r : r + 1, :].astype(f32), 0.0),
                axis=1,
                keepdims=True,
            )
            for r in range(2)
        ],
        axis=0,
    )
    angles = positions * inverse_ref[...]
    cos_table, sin_table = jnp.cos(angles), jnp.sin(angles)
    sin_table = jnp.where(lanes(2 * held) % HD < HD // 2, -sin_table, sin_table)
    fresh = fresh * jnp.tile(cos_table, (1, KVH // 2)) + partner * jnp.tile(
        sin_table, (1, KVH // 2)
    )
    for h in range(KVH):
        cols, odd = pair_cols(h)
        fsend[h] = join(fresh[:held, cols], odd, fresh[held:, cols], not odd)
    send(FRESH)
    send(KV)

    loads = []
    for e in range(local_experts):
        loads.append(pltpu.make_async_copy(gu_hbm.at[e], gu_v.at[e], load_sem.at[0, e]))
    for e in range(local_experts):
        loads.append(pltpu.make_async_copy(dn_hbm.at[e], dn_v.at[e], load_sem.at[1, e]))
    for load in loads:
        load.start()

    pack_step(1)
    pack_cache(1)

    expert_row = lax.broadcasted_iota(jnp.int32, (128, tok), 0)
    for r in range(2):
        dense = jnp.zeros((128, tok), f32)
        for k in range(TOP):
            hit = routes_ref[r, k : k + 1, :] == expert_row
            dense = dense + jnp.where(hit, rw_ref[r, k : k + 1, :], 0.0)
        wrecv[mz, r * tok : (r + 1) * tok, :] = dense.T

    def share_copy(k, slot):
        return pltpu.make_async_remote_copy(
            src_ref=wrecv.at[mz],
            dst_ref=wrecv.at[slot],
            send_sem=zs_sem.at[0, k],
            recv_sem=zr_sem.at[0, k],
            device_id={"req": lax.rem(mz + k, N)},
        )

    def back_copy(r, half, block, to, slot):
        return pltpu.make_async_remote_copy(
            src_ref=psend.at[r, half, other[block]],
            dst_ref=precv.at[r, half, slot],
            send_sem=zs_sem.at[1 + 2 * r + half, block],
            recv_sem=zr_sem.at[1 + 2 * r + half, slot],
            device_id={"req": other[to]},
        )

    def token_copy(r, origin, to, way):
        return pltpu.make_async_remote_copy(
            src_ref=trecv.at[r, origin],
            dst_ref=trecv.at[r, origin],
            send_sem=ts_sem.at[r, way],
            recv_sem=tr_sem.at[r, origin],
            device_id={"req": other[to]},
        )

    def send_tokens(r):
        token_copy(r, mz, 2, 2).start()

        @pl.when(inner)
        def _():
            token_copy(r, mz, 3, 3).start()

        token_copy(r, mz, 1, 1).start()

    def relay_tokens(r):
        token_copy(r, across, 1, 0).wait_recv()

        @pl.when(inner)
        def _():
            token_copy(r, across, 1, 0).start()

    def rest_of_tokens(r):
        token_copy(r, near, 1, 0).wait_recv()
        token_copy(r, mirror, 1, 0).wait_recv()

    def send_back(r, half):
        @pl.when(jnp.logical_not(inner))
        def _():
            back_copy(r, half, 3, 1, 0).start()
            back_copy(r, half, 2, 2, 2).start()

    def send_back_near(r):
        for half in range(2):

            @pl.when(inner)
            def _():
                back_copy(r, half, 1, 1, 1).start()
                back_copy(r, half, 3, 3, 3).start()

            @pl.when(jnp.logical_not(inner))
            def _():
                back_copy(r, half, 1, 1, 1).start()

    def relay_back(r, half):
        @pl.when(inner)
        def _():
            back_copy(r, half, 3, 1, 0).wait_recv()
            both = psend[r, half, across].astype(f32) + precv[r, half, 0].astype(f32)
            psend[r, half, across] = both.astype(bf16)
            back_copy(r, half, 2, 2, 2).start()

    for k in range(1, N):
        share_copy(k, mz).start()

    for r in range(2):
        qrecv[r, me] = qsend[r, me]
        srecv[r, row_at(me, tok), :] = stsend[r, me]
    frecv[row_at(me, held), :] = fsend[me]
    arrive(Q)
    arrive(NEW)
    arrive(FRESH)
    ones = jnp.ones((S * held, lane), bf16)
    spread = jnp.concatenate([frecv[...], ones], axis=1)

    def place_fresh(r):
        wanted = rec_ref[r : r + 1, :]

        def place(i, carry):
            where_to = lax.broadcasted_iota(jnp.int32, (crows, S * held), 0) + i * crows
            hit = jnp.where(where_to == wanted, 1.0, 0.0).astype(bf16)
            both = jnp.dot(hit, spread, preferred_element_type=f32)
            placed[r, i] = both[:, :lane].astype(bf16)
            keep[r, i] = (1.0 - both[:, lane:]).astype(bf16)
            return carry

        lax.fori_loop(0, S, place, 0)

    def pass_on(sent, steps):
        for k in sent:
            exchange(KV, k, me).wait_send()
        send(KV + 1, steps)

    place_fresh(0)
    for k in range(1, 5):
        exchange(KV, k, me).wait_send()
    send(Q1)
    send(NEW1)
    send(KV + 1, (1, 2))

    contract = (((1,), (1,)), ((), ()))

    def key_lanes(r, rows):
        return lanes(rows) < HD if r == 0 else lanes(rows) >= HD

    def chunk(r, state, query, keys, raw, bias=None, mask=None):
        scores = lax.dot_general(query, keys, contract, preferred_element_type=f32)
        if bias is not None:
            scores = scores + bias
        if mask is not None:
            scores = jnp.where(mask, scores, NEG)
        values = jnp.where(key_lanes(r, raw.shape[0]), jnp.ones_like(raw), raw)
        highest = jnp.max(scores, axis=-1, keepdims=True)
        if state is None:
            exps = jnp.exp(scores - highest).astype(bf16)
            return highest, jnp.dot(exps, values, preferred_element_type=f32)
        before, mixed = state
        highest = jnp.maximum(before, highest)
        exps = jnp.exp(scores - highest).astype(bf16)
        mixed = mixed * jnp.exp(before - highest)
        return highest, mixed + jnp.dot(exps, values, preferred_element_type=f32)

    def query_of(r):
        two = qrecv[r, :, :tok, :].reshape(stotal, lane).astype(f32)
        last = qrecv[r, :, tok:, :].reshape(S * half_tok, lane).astype(f32)
        first = two if r == 0 else swap(two)
        second = swap(two) if r == 0 else two
        early = last if r == 0 else swap(last)
        later = swap(last) if r == 0 else last
        third = jnp.concatenate(
            [early.reshape(S, half_tok, lane), later.reshape(S, half_tok, lane)], axis=1
        ).reshape(stotal, lane)
        query = jnp.concatenate([first, second, third], axis=0)
        return jnp.where(key_lanes(r, groups * stotal), query, 0.0).astype(bf16)

    def attend_new(r, query):
        rows = lax.broadcasted_iota(jnp.int32, (groups * stotal, stotal), 0) % stotal
        causal = lax.broadcasted_iota(jnp.int32, (groups * stotal, stotal), 1) <= rows
        return chunk(r, None, query, srecv[r], srecv[r], mask=causal)

    def attend_cache(r, state, query, k):
        source = lax.rem(me + S - k, S)
        raw = kvsend[r, source] if k == 0 else crecv[r, source]
        keys = placed[r, source] + keep[r, source] * raw
        position = lax.broadcasted_iota(jnp.int32, (1, crows), 1) + source * crows
        open_row = (position >= spans_ref[r, 0]) & (position < spans_ref[r, 1])
        return chunk(r, state, query, keys, raw, bias=jnp.where(open_row, 0.0, NEG))

    def finish(r, state):
        mixed = state[1]
        mixed = mixed / swap(mixed)
        turned = swap(mixed)
        low, high = (turned, mixed) if r == 0 else (mixed, turned)
        head = [slice(g * stotal, (g + 1) * stotal) for g in range(groups)]
        two = merge(low[head[0]], high[head[1]]).astype(bf16)
        osend[r, :, :tok, :] = two.reshape(S, tok, lane)
        half = tok // 2
        one_low = low[head[2]].reshape(S, tok, lane)[:, :half].reshape(S * half, lane)
        one_high = high[head[2]].reshape(S, tok, lane)[:, half:].reshape(S * half, lane)
        osend[r, :, tok:, :] = merge(one_low, one_high).astype(bf16).reshape(S, half, lane)
        send(OUT + r)
        orecv[r, me] = osend[r, me]

    def gather_heads(r):
        arrive(OUT + r)
        for p in range(S // 2):
            even, odd = orecv[r, 2 * p].astype(f32), orecv[r, 2 * p + 1].astype(f32)
            even_solo, odd_solo = even[tok:], odd[tok:]
            odd_two = swap(odd[:tok])
            tile_b = merge(jnp.concatenate([even_solo, swap(even_solo)], axis=0), odd_two)
            tile_c = merge(odd_two, jnp.concatenate([swap(odd_solo), odd_solo], axis=0))
            att[r, :, p * 3 * lane : (p + 1) * 3 * lane] = jnp.concatenate(
                [even[:tok], tile_b, tile_c], axis=1
            )
        attended = att[r]
        mean_square = jnp.mean(attended * attended, axis=-1, keepdims=True)
        gain = gain_ref[...].reshape(1, width)
        trecv[r, mz] = (attended * lax.rsqrt(mean_square + 1e-06) * gain).astype(bf16)
        send_tokens(r)

    query = query_of(0)
    state = attend_new(0, query)
    state = attend_cache(0, state, query, 0)
    pass_on(range(5, S), (3, 4))
    arrive(KV)
    for k in range(1, S):
        state = attend_cache(0, state, query, k)
    finish(0, state)
    send(KV + 1, range(5, S))

    place_fresh(1)
    arrive(Q1)
    arrive(NEW1)
    query = query_of(1)
    state = attend_new(1, query)
    state = attend_cache(1, state, query, 0)
    for part in ((1, 2), (3, 4), (5, 6, 7)):
        for k in part:
            arrive_from(KV + 1, k)
        for k in part:
            state = attend_cache(1, state, query, k)
        if part[0] == 1:
            gather_heads(0)
    finish(1, state)
    relay_tokens(0)
    gather_heads(1)
    rest_of_tokens(0)
    for k in range(1, N):
        share_copy(k, lax.rem(mz + N - k, N)).wait_recv()

    rows_total = N * tok
    part_width = width // 2

    def experts(r):
        tokens = trecv[r].reshape(rows_total, width)
        weights = wrecv[:, r * tok : (r + 1) * tok, :].reshape(rows_total, 128)
        column = lax.broadcasted_iota(jnp.int32, weights.shape, 1)
        for e in range(local_experts):
            if r == 0:
                loads[e].wait()
            hidden = jnp.dot(tokens, gu_v[e], preferred_element_type=f32)
            gate, up = hidden[:, :FF], hidden[:, FF:]
            share = jnp.sum(
                jnp.where(column == mz * local_experts + e, weights, 0.0), axis=1, keepdims=True
            )
            act[:, e * FF : (e + 1) * FF] = (gate / (1.0 + jnp.exp(-gate)) * up * share).astype(
                bf16
            )
        if r == 0:
            for load in loads[local_experts:]:
                load.wait()
        down = dn_v[...].reshape(local_experts * FF, width)
        for half in range(2):
            summed = jnp.dot(
                act[...],
                down[:, half * part_width : (half + 1) * part_width],
                preferred_element_type=f32,
            )
            psend[r, half] = summed.astype(bf16).reshape(N, tok, part_width)
            send_back(r, half)
        send_back_near(r)

    experts(0)
    relay_tokens(1)
    for half in range(2):
        relay_back(0, half)
    rest_of_tokens(1)
    experts(1)
    for half in range(2):
        relay_back(1, half)
    for r in range(2):
        for half in range(2):
            cols = slice(half * part_width, (half + 1) * part_width)
            back_copy(r, half, 1, 1, 1).wait_recv()
            back_copy(r, half, 2, 2, 2).wait_recv()
            mixture = att[r, :, cols] + psend[r, half, mz].astype(f32)
            mixture = mixture + precv[r, half, 1].astype(f32) + precv[r, half, 2].astype(f32)
            total[r, :, cols] = mixture

            @pl.when(inner)
            def _():
                back_copy(r, half, 3, 3, 3).wait_recv()
                total[r, :, cols] += precv[r, half, 3].astype(f32)

            out_ref[r * tok : (r + 1) * tok, cols] = total[r, :, cols].astype(bf16)
    for kind in (Q, NEW, FRESH, KV + 1, OUT, OUT + 1, Q1, NEW1):
        for k in range(1, S):
            exchange(kind, k, me).wait_send()
    for k in range(1, N):
        share_copy(k, mz).wait_send()
    for r in range(2):
        for half in range(2):
            for block in (1, 2, 3):
                back_copy(r, half, block, 1, 1).wait_send()
        for way in (1, 2):
            token_copy(r, mz, 1, way).wait_send()

        @pl.when(inner)
        def _():
            token_copy(r, mz, 3, 3).wait_send()
            token_copy(r, across, 1, 0).wait_send()


def head_parallel_body(
    queries,
    new_kv,
    cache_kv,
    cache_spans,
    recompute_rows,
    held_states,
    key_weight,
    norm_gain,
    routes,
    route_weights,
    expert_gate_up,
    expert_down,
):
    S = lax.axis_size("seq")
    N = lax.axis_size("req")
    req_rows, tok, width = queries.shape
    crows = cache_kv.shape[2]
    held = held_states.shape[1]
    local_experts = expert_gate_up.shape[0]
    groups = H // KVH
    bf16, f32 = jnp.bfloat16, jnp.float32
    half = HD // 2
    inverse = THETA ** (-((np.arange(2 * HD) % half) * (2.0 / HD)))
    inverse = jnp.asarray(inverse.astype(np.float32).reshape(1, 2 * HD))
    vmem = pl.BlockSpec(memory_space=pltpu.VMEM)
    smem = pl.BlockSpec(memory_space=pltpu.SMEM)
    hbm = pl.BlockSpec(memory_space=pl.ANY)
    lane = 2 * HD
    rows = req_rows * tok
    out = pl.pallas_call(
        layer_kernel,
        out_shape=pltpu.VMEM((rows, width), bf16),
        in_specs=[smem] + [vmem] * 5 + [hbm] * 7,
        out_specs=vmem,
        scratch_shapes=[
            pltpu.VMEM((req_rows, tok, width), bf16),
            pltpu.VMEM((2, req_rows, tok, KVH * HD), bf16),
            pltpu.VMEM((req_rows, 2, crows, KVH * HD), bf16),
            pltpu.VMEM((req_rows * held, width), bf16),
            pltpu.VMEM(key_weight.shape, bf16),
            pltpu.VMEM(expert_gate_up.shape, bf16),
            pltpu.VMEM(expert_down.shape, bf16),
            pltpu.VMEM((2, S, crows, lane), bf16),
            pltpu.VMEM((2, S, tok, lane), bf16),
            pltpu.VMEM((2, S, tok * 3 // 2, lane), bf16),
            pltpu.VMEM((S, held, lane), bf16),
            pltpu.VMEM((2, S, tok * 3 // 2, lane), bf16),
            pltpu.VMEM((2, S, crows, lane), bf16),
            pltpu.VMEM((2, S * tok, lane), bf16),
            pltpu.VMEM((2, S, tok * 3 // 2, lane), bf16),
            pltpu.VMEM((S * held, lane), bf16),
            pltpu.VMEM((2, S, tok * 3 // 2, lane), bf16),
            pltpu.VMEM((2, S, crows, lane), bf16),
            pltpu.VMEM((2, S, crows, lane), bf16),
            pltpu.VMEM((2, tok, width), f32),
            pltpu.VMEM((2, N, tok, width), bf16),
            pltpu.VMEM((N, rows, 128), f32),
            pltpu.VMEM((N * tok, local_experts * FF), bf16),
            pltpu.VMEM((2, tok, width), f32),
            pltpu.VMEM((2, 2, N, tok, width // 2), bf16),
            pltpu.VMEM((2, 2, N, tok, width // 2), bf16),
            pltpu.SemaphoreType.DMA((6,)),
            pltpu.SemaphoreType.DMA((2, local_experts)),
            pltpu.SemaphoreType.DMA((9, S)),
            pltpu.SemaphoreType.DMA((9, S)),
            pltpu.SemaphoreType.DMA((5, N)),
            pltpu.SemaphoreType.DMA((5, N)),
            pltpu.SemaphoreType.DMA((2, N)),
            pltpu.SemaphoreType.DMA((2, N)),
        ],
        compiler_params=pltpu.CompilerParams(
            collective_id=0, has_side_effects=True, vmem_limit_bytes=60 << 20
        ),
        name="layer",
    )(
        cache_spans,
        recompute_rows,
        inverse,
        norm_gain,
        jnp.transpose(routes, (0, 2, 1)),
        jnp.transpose(route_weights, (0, 2, 1)),
        queries,
        new_kv,
        cache_kv,
        held_states.reshape(req_rows * held, width),
        key_weight,
        expert_gate_up,
        expert_down,
    )
    return out.reshape(req_rows, tok, width)


def solution(mesh):
    by_heads = mesh.shape["seq"] == KVH and mesh.shape["req"] == 4
    body = head_parallel_body if by_heads else body_wide
    in_specs = (
        P("req", "seq", None),
        P(None, "req", "seq", None),
        P(None, "req", "seq", None),
        P("req", None),
        P("req", None),
        P("req", "seq", None),
        P(),
        P(),
        P("req", "seq", None),
        P("req", "seq", None),
        P("req", None, None),
        P("req", None, None),
    )
    out_specs = P("req", "seq", None)
    return jax.shard_map(body, mesh=mesh, in_specs=in_specs, out_specs=out_specs, check_vma=False)
```
